256 devices in a mesh: tok: 32 (over z_lo, y, core), col: 8 (over x, z_hi).
Axes of the slice: x: 4, y: 4, z: 8 (z_hi: 2, z_lo: 4; z = z_hi * 4 + z_lo), core: 2. Of those that a mesh axis runs over, the one named last changes fastest.
Arguments:
- hidden: bfloat16 [8192, 8192], P('tok'), may hold values from -6 to 6
- norm_gain: float32 [8192], replicated, may hold values from 0.1 to 1.9
- token_ids: int32 [8192], P('tok'), may hold values from 0 to 128000, as said below
- owner: int32 [1], replicated, may hold values from 0 to 31
- query_store: bfloat16 [32, 8192, 4096], P('tok', None, 'col'), may hold values from -0.0625 to 0.0625
- key_store: bfloat16 [32, 8192, 512], P('tok', None, 'col'), may hold values from -0.0625 to 0.0625
Outputs:
- queries: bfloat16 [8192, 4096], P('tok', 'col')
- keys: bfloat16 [8192, 512], P('tok', 'col')
- hessian: float32 [8192, 8192], P('col', 'tok')
The draws below stay inside these ranges and needn't reach their ends.
Inputs may be any that keep to these rules, and one draw needn't show every extreme that they name: `token_ids`: id 128000 marks the first token of a document; every other id is below it.
All inputs are finite; a program needn't handle non-finite values.
Results may differ from the reference program's by a relative error of at most 0.0049.
Values may be sent and summed in bfloat16 or wider, within the bound.
No kernel may reach another device: no remote copies, remote signals or barrier semaphores. Data moves between devices by JAX's collectives and lax.ppermute only.
A program may use at most 128 MiB of HBM per device.

```python
import jax
import jax.numpy as jnp
from jax import lax

D = 8192
HEAD = 128
SEQ = 128
QCOLS = 4096
KCOLS = 512
TOKENS = 8192
LAYERS = 32
N_TOK = 32


def draw_token_ids(key, part):
    base = jax.random.fold_in(key, 11)
    first_key, second_key = jax.random.split(base)
    marks = jax.random.randint(first_key, (TOKENS,), 0, 32) == 0
    words = jax.random.randint(second_key, (TOKENS,), 0, 128000)
    return jnp.where(marks, 128000, words).astype(jnp.int32)


def block_levels(rng, shape, shards, least, high):
    loudness, own = 1.0, jax.random.fold_in(rng, 6)
    for axis_at, blocks in shards:
        heights = jnp.exp(jax.random.uniform(jax.random.fold_in(own, axis_at), (blocks,), jnp.float32, least / len(shards), high / len(shards)))
        loudness = loudness * jnp.repeat(heights, shape[axis_at] // blocks).reshape([-1 if axis == axis_at else 1 for axis in range(len(shape))])
    return loudness


def normal_values(stream_key, extent, scale, reach, cuts=(), kind=jnp.bfloat16):
    array = scale * jax.random.normal(stream_key, extent, jnp.float32)
    if cuts:
        array = array * block_levels(stream_key, extent, cuts, -0.22, 0.18)
    return jnp.clip(array, -reach, reach).astype(kind)


def setup_inputs(seed: int = 0) -> dict:
    splits = jax.random.split(jax.random.key(seed), 7)
    return {
        "hidden": normal_values(splits[0], (TOKENS, D), 1.0, 6.0, ((0, 32),)),
        "norm_gain": jnp.clip(1.0 + 0.18 * jax.random.normal(splits[1], (D,), jnp.float32), 0.1, 1.9),
        "token_ids": draw_token_ids(jax.random.fold_in(splits[6], 71), 0),
        "owner": jax.random.randint(splits[3], (1,), 0, N_TOK).astype(jnp.int32),
        "query_store": normal_values(splits[4], (LAYERS, D, QCOLS), D ** -0.5, 0.0625, ((0, 32), (2, 8))),
        "key_store": normal_values(splits[5], (LAYERS, D, KCOLS), D ** -0.5, 0.0625, ((0, 32), (2, 8))),
    }


begin_token = 128000
rope_base = 500000.0

def positions(token_ids):
    samples = token_ids.reshape(-1, SEQ)
    index = jnp.arange(SEQ, dtype=jnp.int32)
    starts = jnp.where(samples == begin_token, index[None, :], jnp.zeros_like(samples))
    latest = lax.cummax(starts, axis=1)
    return (index[None, :] - latest).reshape(-1)

def rotate(values, place, start):
    width = values.shape[1]
    dims = (start + jnp.arange(width, dtype=jnp.int32)) % HEAD
    pair = (dims[0::2] // 2).astype(jnp.float32)
    freq = jnp.power(jnp.float32(rope_base), -2.0 * pair / HEAD)
    angle = place.astype(jnp.float32)[:, None] * freq[None, :]
    cosine = jnp.cos(angle)
    sine = jnp.sin(angle)
    even = values[:, 0::2]
    odd = values[:, 1::2]
    first = even * cosine - odd * sine
    second = even * sine + odd * cosine
    return jnp.stack([first, second], axis=-1).reshape(values.shape[0], width)

def normalize(hidden, norm_gain):
    wide = hidden.astype(jnp.float32)
    meansq = lax.optimization_barrier(jnp.mean(wide * wide, axis=-1, keepdims=True))
    return (wide * lax.rsqrt(meansq + 1e-05) * norm_gain[None, :]).astype(jnp.bfloat16)

def reference(hidden, norm_gain, token_ids, owner, query_store, key_store):
    normed = normalize(hidden, norm_gain)
    place = positions(token_ids)
    slot = owner[0].astype(jnp.int32)
    weight_q = lax.dynamic_index_in_dim(query_store, slot, 0, keepdims=False)
    weight_k = lax.dynamic_index_in_dim(key_store, slot, 0, keepdims=False)
    raw_q = jnp.dot(normed, weight_q, preferred_element_type=jnp.float32)
    raw_k = jnp.dot(normed, weight_k, preferred_element_type=jnp.float32)
    queries = rotate(raw_q, place, 0).astype(jnp.bfloat16)
    keys = rotate(raw_k, place, 0).astype(jnp.bfloat16)
    gram = lax.dot_general(normed, normed, (((0,), (0,)), ((), ())), preferred_element_type=jnp.float32)
    hessian = gram * (2.0 / TOKENS)
    return (queries, keys, hessian)
```

```python
import jax
import jax.numpy as jnp
import numpy as np
from jax import lax
from jax.sharding import Mesh, PartitionSpec as P

HEAD = 128
SEQ = 128


begin_token = 128000
rope_base = 500000.0

NY, NZ = 4, 4
TOK = ("zl", "y", "k")
COL = ("x", "zh")


def ring(n, shift):
    return [(i, (i + shift) % n) for i in range(n)]


def send(array, axis, shift):
    n = {"y": NY, "zl": NZ, "k": 2}[axis]
    return lax.ppermute(array, axis, ring(n, shift % n))


def pick(array, index, axis=0):
    return lax.dynamic_index_in_dim(array, index, axis, keepdims=False)


def positions(token_ids):
    samples = token_ids.reshape(-1, SEQ)
    index = jnp.arange(SEQ, dtype=jnp.int32)
    starts = jnp.where(samples == begin_token, index[None, :], 0)
    seen = index[None, :] <= index[:, None]
    latest = jnp.max(jnp.where(seen[None], starts[:, None, :], 0), axis=2)
    return (index[None, :] - latest).reshape(-1)


def rotate(values, place):
    width = values.shape[1]
    dims = jnp.arange(HEAD, dtype=jnp.int32)
    pair = (dims // 2).astype(jnp.float32)
    freq = jnp.power(jnp.float32(rope_base), -2.0 * pair / HEAD)
    angle = place.astype(jnp.float32)[:, None] * freq[None, :]
    cosine = jnp.cos(angle)
    sine = jnp.sin(angle)
    turn = np.zeros((HEAD, HEAD), np.float32)
    turn[np.arange(1, HEAD, 2), np.arange(0, HEAD, 2)] = -1.0
    turn[np.arange(0, HEAD, 2), np.arange(1, HEAD, 2)] = 1.0
    span = min(width, HEAD)
    out = []
    for start in range(0, width, span):
        block = values[:, start : start + span]
        other = jnp.dot(
            block,
            jnp.asarray(turn[:span, :span]),
            precision=lax.Precision.HIGHEST,
            preferred_element_type=jnp.float32,
        )
        out.append((block, other))
    return out, cosine, sine


def normalize(hidden, norm_gain):
    wide = hidden.astype(jnp.float32)
    meansq = jnp.mean(wide * wide, axis=-1, keepdims=True)
    return (wide * lax.rsqrt(meansq + 1e-05) * norm_gain[None, :]).astype(jnp.bfloat16)


def gram(left, right):
    return lax.dot_general(
        left, right, (((0,), (0,)), ((), ())), preferred_element_type=jnp.float32
    )


def shards(hidden, norm_gain, token_ids, owner, query_store, key_store):
    y, z, k = lax.axis_index("y"), lax.axis_index("zl"), lax.axis_index("k")
    column = lax.axis_index("x") * 2 + lax.axis_index("zh")
    root = owner[0]
    root_z, root_y, root_k = root // 8, (root // 2) % 4, root % 2

    tokens, depth = hidden.shape
    half = depth // 2
    piece = half // (NY * NZ)
    qwidth, kwidth = query_store.shape[2], key_store.shape[2]

    q = query_store[0].reshape(2, NY, NZ, piece, qwidth)
    kt = key_store[0].T.reshape(2, kwidth // 2, 2, NY, NZ, piece)
    kt = kt.transpose(2, 3, 4, 1, 0, 5).reshape(2, NY, NZ, kwidth // 2, 2 * piece)
    packed = jnp.concatenate([q, kt], axis=3)
    away = pick(packed, 1 - k)
    home = pick(packed, k)
    there = send(away, "k", 1)
    mine = jnp.where(root_k == k, home, there)

    step_y = (y - root_y) % NY
    h = NZ // 2
    far = pick(mine, (y + 2) % NY)
    a = send(far[:h], "y", 1)
    b = send(far[h:], "y", -1)
    up = pick(mine, (y + 1) % NY)
    down = pick(mine, (y + 3) % NY)
    up = jnp.concatenate([jnp.where(step_y == 1, a, up[:h]), up[h:]], axis=0)
    down = jnp.concatenate([down[:h], jnp.where(step_y == 3, b, down[h:])], axis=0)
    c = send(up, "y", 1)
    d = send(down, "y", -1)
    own = pick(mine, y)
    low = jnp.where(step_y == 0, own[:h], jnp.where(step_y == 3, d[:h], c[:h]))
    high = jnp.where(step_y == 0, own[h:], jnp.where(step_y == 1, c[h:], d[h:]))
    quarter = jnp.concatenate([low, high], axis=0)

    normed = normalize(hidden, norm_gain)
    other = send(normed, "k", 1)
    both = jnp.concatenate([normed, other], axis=0)

    row_width = depth // 8
    tile = depth // (NY * NZ * 2)
    rows = lax.dynamic_slice_in_dim(both, column * row_width, row_width, 1)
    cols = both.reshape(2 * tokens, NZ, NY, 2, tile)
    cols = pick(cols, k, 3).transpose(0, 2, 1, 3)

    def part(rel):
        block = pick(cols, (y + rel) % NY, 1)
        return gram(block.reshape(2 * tokens, NZ * tile), rows).reshape(NZ, tile, row_width)

    bf = jnp.bfloat16
    p2 = part(2).astype(bf)
    p2, quarter = lax.optimization_barrier((p2, quarter))
    ga = send(p2[:h], "y", 1)
    gb = send(p2[h:], "y", -1)
    p1, p3, p0 = part(1), part(3), part(0)
    p1 = jnp.concatenate([p1[:h] + ga.astype(jnp.float32), p1[h:]], axis=0).astype(bf)
    p3 = jnp.concatenate([p3[:h], p3[h:] + gb.astype(jnp.float32)], axis=0).astype(bf)
    gc = send(p1, "y", 1)
    gd = send(p3, "y", -1)

    step_z = (z - root_z) % NZ
    got = [pick(quarter, z)]
    for s in (1, 2, 3):
        got.append(send(pick(quarter, (z + s) % NZ), "zl", s))
    seed = got[0]
    for s in (1, 2, 3):
        seed = jnp.where(step_z == s, got[s], seed)
    strip = [seed] + [send(seed, "zl", -s) for s in (1, 2, 3)]
    strip = jnp.stack(strip, axis=0)

    total = p0 + gc.astype(jnp.float32) + gd.astype(jnp.float32)
    strip, total = lax.optimization_barrier((strip, total))

    left = send(strip, "y", 1)
    right = send(strip, "y", -1)
    fl = send(left[:h], "y", 1)
    fr = send(right[h:], "y", -1)
    weights = jnp.stack([strip, right, jnp.concatenate([fl, fr], axis=0), left], axis=0)

    totalb = total.astype(bf)
    hess = pick(total, z)
    for s in (1, 2, 3):
        hess = hess + send(pick(totalb, (z + s) % NZ), "zl", s).astype(jnp.float32)
    all_tokens = tokens * NY * NZ * 2
    hessian = hess.T * (2.0 / all_tokens)

    def order(x):
        x = lax.dynamic_slice_in_dim(x, k * half, half, 1).reshape(-1, NY, NZ, piece)
        x = jnp.concatenate([x, x], axis=1)
        x = lax.dynamic_slice_in_dim(x, y, NY, 1)
        x = jnp.concatenate([x, x], axis=2)
        x = lax.dynamic_slice_in_dim(x, z, NZ, 2)
        return x.reshape(-1, half)

    lhs = order(both)
    wq = weights[:, :, :piece].reshape(half, qwidth)
    wk = weights[:, :, piece:].reshape(NY * NZ, kwidth // 2, 2, piece)
    wk = wk.transpose(2, 1, 0, 3).reshape(kwidth, half)
    raw_q = jnp.dot(lhs, wq, preferred_element_type=jnp.float32)
    raw_k = lax.dot_general(
        lhs, wk, (((1,), (1,)), ((), ())), preferred_element_type=jnp.float32
    )
    raw = jnp.concatenate([raw_q, raw_k], axis=1)
    raw = raw[:tokens] + send(raw[tokens:], "k", 1)

    place = positions(token_ids)
    blocks, cosine, sine = rotate(raw[:, :qwidth], place)
    queries = jnp.concatenate([u * cosine + v * sine for u, v in blocks], axis=1)
    blocks, cosine, sine = rotate(raw[:, qwidth:], place)
    offset = (column * kwidth) % HEAD
    cosine = lax.dynamic_slice_in_dim(cosine, offset, kwidth, 1)
    sine = lax.dynamic_slice_in_dim(sine, offset, kwidth, 1)
    keys = jnp.concatenate([u * cosine + v * sine for u, v in blocks], axis=1)
    return (queries.astype(bf), keys.astype(bf), hessian)


def solution(mesh):
    fine = Mesh(mesh.devices.reshape(NZ, NY, 2, 4, 2), ("zl", "y", "k", "x", "zh"))
    placed = (P(TOK, None), P(), P(TOK), P(), P(TOK, None, COL), P(TOK, None, COL))
    return jax.shard_map(
        shards,
        mesh=fine,
        in_specs=placed,
        out_specs=(P(TOK, COL), P(TOK, COL), P(COL, TOK)),
        check_vma=False,
    )
```

```python
import functools

import jax
import jax.numpy as jnp
from jax import lax
from jax.experimental import pallas as pl
from jax.experimental.pallas import tpu as pltpu
from jax.sharding import Mesh, PartitionSpec as P

HEAD = 128
SEQ = 128


begin_token = 128000
rope_base = 500000.0

NY, NZ, NC = 4, 4, 8
TOK = ("zl", "y", "k")
COL = ("x", "zh")
ALL = TOK + COL
SIZES = {"y": NY, "zl": NZ, "k": 2}
f32, bf16 = jnp.float32, jnp.bfloat16


def send(array, axis, shift):
    n = SIZES[axis]
    return lax.ppermute(array, axis, [(i, (i + shift) % n) for i in range(n)])


together = lax.optimization_barrier


def pick(array, index):
    return lax.dynamic_index_in_dim(array, index, 0, keepdims=False)


def positions(token_ids):
    samples = token_ids.reshape(-1, SEQ)
    index = jnp.arange(SEQ, dtype=jnp.int32)
    starts = jnp.where(samples == begin_token, index[None, :], 0)
    seen = index[None, :] <= index[:, None]
    latest = jnp.max(jnp.where(seen[None], starts[:, None, :], 0), axis=2)
    return (index[None, :] - latest).reshape(-1)


def turns(place):
    dims = jnp.arange(HEAD, dtype=jnp.int32)
    pair = (dims // 2).astype(f32)
    freq = jnp.power(f32(rope_base), -2.0 * pair / HEAD)
    angle = place.astype(f32)[:, None] * freq[None, :]
    sign = jnp.where(dims % 2 == 0, -1.0, 1.0).astype(f32)
    return jnp.cos(angle), jnp.sin(angle) * sign[None, :]


def normalize(hidden, norm_gain):
    wide = hidden.astype(f32)
    meansq = jnp.mean(wide * wide, axis=-1, keepdims=True)
    return (wide * lax.rsqrt(meansq + 1e-05) * norm_gain[None, :]).astype(bf16)


def across(left, right):
    return lax.dot_general(left, right, (((0,), (0,)), ((), ())), preferred_element_type=f32)


def gram_body(role, table, *refs):
    ca, cb, r0a, r0b, r1a, r1b = (ref[...] for ref in refs[:6])
    rest = refs[6:]
    slot = pl.program_id(0)
    half = NZ // 2
    ta, tb = ca.T, cb.T
    dot = functools.partial(jnp.dot, preferred_element_type=f32)
    tile = jnp.concatenate([dot(ta, r0a) + dot(tb, r0b), dot(ta, r1a) + dot(tb, r1b)], axis=1)
    if role == "far":
        low, high = rest

        @pl.when(slot < half)
        def _():
            low[0] = tile.astype(bf16)

        @pl.when(slot >= half)
        def _():
            high[0] = tile.astype(bf16)

    elif role in ("up", "down"):
        add, out = rest
        use = slot < half if role == "up" else slot >= half
        out[0] = (tile + jnp.where(use, add[0].astype(f32), 0.0)).astype(bf16)
    else:
        first, second, own, others = rest
        tile = tile + first[0].astype(f32) + second[0].astype(f32)

        @pl.when(slot == 0)
        def _():
            own[...] = tile

        @pl.when(slot > 0)
        def _():
            others[0] = tile.astype(bf16)


def gram(role, table, mine, other, *adds):
    tokens, depth = mine.shape
    tile = depth // (NY * NZ * 2)
    half = NZ // 2
    at = lambda row: pl.BlockSpec((tokens, tile), lambda s, tab: (0, tab[row, s]))
    block = (1, tile, 2 * tile)
    low = lambda s, tab: (jnp.minimum(s, half - 1), 0, 0)
    high = lambda s, tab: (jnp.maximum(s - half, 0), 0, 0)
    every = lambda s, tab: (s, 0, 0)
    shape = lambda n, kind: jax.ShapeDtypeStruct((n, tile, 2 * tile), kind)
    ins = [at(0), at(0), at(1), at(1), at(2), at(2)]
    if role == "far":
        outs = [pl.BlockSpec(block, low), pl.BlockSpec(block, high)]
        shapes = [shape(half, bf16), shape(half, bf16)]
    elif role in ("up", "down"):
        ins.append(pl.BlockSpec(block, low if role == "up" else high))
        outs, shapes = pl.BlockSpec(block, every), shape(NZ, bf16)
    else:
        ins += [pl.BlockSpec(block, every)] * 2
        outs = [
            pl.BlockSpec((tile, 2 * tile), lambda s, tab: (0, 0)),
            pl.BlockSpec(block, lambda s, tab: (jnp.maximum(s - 1, 0), 0, 0)),
        ]
        shapes = [jax.ShapeDtypeStruct((tile, 2 * tile), f32), shape(NZ - 1, bf16)]
    return pl.pallas_call(
        functools.partial(gram_body, role),
        grid_spec=pltpu.PrefetchScalarGridSpec(
            num_scalar_prefetch=1, grid=(NZ,), in_specs=ins, out_specs=outs
        ),
        out_shape=shapes,
        cost_estimate=pl.CostEstimate(
            flops=2 * 2 * tokens * 2 * tile * tile * NZ,
            bytes_accessed=8 * NZ * tokens * tile * 2,
            transcendentals=0,
        ),
        name="gram_" + role,
    )(table, mine, other, mine, other, mine, other, *adds)


def project_body(fresh, table, ma, mb, w, *refs):
    out = refs[-1]

    @pl.when(pl.program_id(0) == 0)
    def _():
        out[...] = jnp.zeros_like(out) if fresh else refs[0][...]

    out[0] += jnp.dot(ma[...], w[0], preferred_element_type=f32)
    out[1] += jnp.dot(mb[...], w[0], preferred_element_type=f32)


def project(table, mine, other, weights, sofar=None):
    tokens = mine.shape[0]
    n, piece, width = weights.shape
    at = pl.BlockSpec((tokens, piece), lambda s, tab: (0, tab[s]))
    whole = pl.BlockSpec((2, tokens, width), lambda s, tab: (0, 0, 0))
    fresh = sofar is None
    return pl.pallas_call(
        functools.partial(project_body, fresh),
        grid_spec=pltpu.PrefetchScalarGridSpec(
            num_scalar_prefetch=1,
            grid=(n,),
            in_specs=[at, at, pl.BlockSpec((1, piece, width), lambda s, tab: (s, 0, 0))]
            + ([] if fresh else [whole]),
            out_specs=whole,
        ),
        out_shape=jax.ShapeDtypeStruct((2, tokens, width), f32),
        cost_estimate=pl.CostEstimate(
            flops=4 * tokens * piece * width * n,
            bytes_accessed=n * (2 * tokens * piece + piece * width) * 2 + 16 * tokens * width,
            transcendentals=0,
        ),
        name="project",
    )(table, mine, other, weights, *([] if fresh else [sofar]))


def rope_body(a, b, cosine, sine, out):
    even = lax.broadcasted_iota(jnp.int32, cosine.shape, 1) % 2 == 0
    for start in range(0, a.shape[1], HEAD):
        span = pl.ds(start, HEAD)
        x = a[:, span] + b[:, span]
        swapped = jnp.where(even, pltpu.roll(x, HEAD - 1, 1), pltpu.roll(x, 1, 1))
        out[:, span] = (x * cosine[...] + swapped * sine[...]).astype(out.dtype)


def rope(a, b, cosine, sine):
    return pl.pallas_call(
        rope_body, out_shape=jax.ShapeDtypeStruct(a.shape, bf16), name="rope"
    )(a, b, cosine, sine)


def assemble_body(scale, slots, own, r0, r1, extra, out):
    tile = out.shape[1]

    def put(n, value):
        out[pl.ds(pl.multiple_of(slots[n] * tile, tile), tile), :] = value * scale

    put(0, r1[...].astype(f32))
    put(1, extra[...])
    put(2, r0[...].astype(f32))
    put(3, own[:, :tile].T)
    put(4, own[:, tile:].T)


def assemble(scale, slots, own, r0, r1, extra):
    tile = own.shape[0]
    return pl.pallas_call(
        functools.partial(assemble_body, scale),
        in_specs=[pl.BlockSpec(memory_space=pltpu.SMEM)] + [pl.BlockSpec(memory_space=pltpu.VMEM)] * 4,
        out_shape=jax.ShapeDtypeStruct((4 * tile, tile), f32),
        name="assemble",
    )(slots, own, r0, r1, extra)


def row_pair(t, c):
    u, m = t // 4, t % 4
    p = (t + (c > u)) % 2
    return jnp.where(c == u, m, p), jnp.where(c == u, (m + 1) % 4, p + 2)


def partner_moves(q):
    moves = []
    for t in range(NY * NZ * 2):
        for c in range(NC):
            u, m = t // 4, t % 4
            if c == u:
                r = (m + 1) % 4 if q == 0 else m
            else:
                r = (t + (c > u)) % 2 + 2 * ((q + m // 2) % 2)
            moves.append((t * NC + c, (4 * c + r) * NC + u))
    return moves


def shards(hidden, norm_gain, token_ids, owner, query_store, key_store):
    y, z, k = lax.axis_index("y"), lax.axis_index("zl"), lax.axis_index("k")
    column = lax.axis_index("x") * 2 + lax.axis_index("zh")
    root = owner[0]
    root_z, root_y, root_k = root // 8, (root // 2) % 4, root % 2

    tokens, depth = hidden.shape
    half = depth // 2
    piece = half // (NY * NZ)
    qwidth, kwidth = query_store.shape[2], key_store.shape[2]
    h = NZ // 2
    here = root_k == k

    q = query_store[0].reshape(2 * NY, NZ * piece, qwidth)

    def block(rel, here):
        at = (y + rel) % NY
        there = send(pick(q, (1 - k) * NY + at), "k", 1)
        return jnp.where(here, pick(q, k * NY + at), there)

    step_y = (y - root_y) % NY
    far = block(2, here).reshape(2, h * piece, qwidth)
    far, then = together((far, here))
    a = send(far[0], "y", 1)
    b = send(far[1], "y", -1)
    up = block(1, then).reshape(2, h * piece, qwidth)
    down = block(3, then).reshape(2, h * piece, qwidth)
    c = send(jnp.where(step_y == 1, a[None], up), "y", 1)
    d = send(jnp.where(step_y == 3, b[None], down), "y", -1)
    own = block(0, then).reshape(2, h * piece, qwidth)
    low = lax.broadcasted_iota(jnp.int32, (2, 1, 1), 0) == 0
    from_c = (step_y == 1) | ((step_y == 2) & low)
    quarter = jnp.where(step_y == 0, own, jnp.where(from_c, c, d))
    quarter = quarter.reshape(NZ, piece, qwidth)

    kt = key_store[0].T.reshape(kwidth, 2, half)
    away = jnp.where(k == 0, kt[:, 1], kt[:, 0])
    home = jnp.where(k == 0, kt[:, 0], kt[:, 1])
    wk = jnp.where(here, home, send(away, "k", 1))
    wk = lax.psum(jnp.where((step_y == 0) & (z == root_z), wk, 0), ("zl", "y"))

    mine = normalize(hidden, norm_gain)
    other = send(mine, "k", 1)

    zs = (z + jnp.arange(NZ)) % NZ

    def table(rel):
        t = zs * (2 * NY) + ((y + rel) % NY) * 2 + k
        r0, r1 = row_pair(t, column)
        return jnp.stack([t, 4 * column + r0, 4 * column + r1]).astype(jnp.int32)

    tile = depth // (NY * NZ * 2)
    both = [lax.dynamic_slice_in_dim(x, (4 * column + k) * tile, 3 * tile, 1) for x in (mine, other)]
    extra = sum(across(x[:, :tile], x[:, 2 * tile :]) for x in both)
    p_low, p_high = gram("far", table(2), mine, other)
    p_low, p_high, quarter, extra = together((p_low, p_high, quarter, extra))
    extra = lax.psum(extra, ("zl", "y"))
    ga = send(p_low, "y", 1)
    gb = send(p_high, "y", -1)
    gc = send(gram("up", table(1), mine, other, ga), "y", 1)
    gd = send(gram("down", table(3), mine, other, gb), "y", -1)

    step_z = (z - root_z) % NZ
    seed = pick(quarter, z)
    for s in (1, 2, 3):
        got = send(pick(quarter, (z + s) % NZ), "zl", s)
        seed = jnp.where(step_z == s, got, seed)
    strip = jnp.stack([seed] + [send(seed, "zl", -s) for s in (1, 2, 3)], axis=0)

    hess, rest = gram("own", table(0), mine, other, gc, gd)
    strip, hess, rest = together((strip, hess, rest))

    def depth_tiles(rel):
        return (k * NY * NZ + ((y + rel) % NY) * NZ + zs).astype(jnp.int32)

    left = send(strip, "y", 1)
    right = send(strip, "y", -1)
    raw = project(depth_tiles(0), mine, other, strip)
    parts = [send(rest[s - 1], "zl", s) for s in (1, 2, 3)]
    left, right, parts, extra, wk, raw = together((left, right, parts, extra, wk, raw))
    fl = send(left[:h], "y", 1)
    fr = send(right[h:], "y", -1)

    for part in parts:
        hess = hess + part.astype(f32)
    t = z * (2 * NY) + y * 2 + k
    u, m = t // 4, t % 4
    diagonal = column == u
    r0, r1 = row_pair(t, column)
    tiles = hess.astype(bf16)
    tiles = [tiles[:, :tile], tiles[:, tile:]]
    mirrored = []
    for n in (0, 1):
        second = jnp.where(diagonal, 1, (n + m // 2) % 2) == 1
        mirrored.append(lax.ppermute(jnp.where(second, tiles[1], tiles[0]), ALL, partner_moves(n)))
    missing = 1 - r0 % 2
    slot0 = jnp.where(diagonal, (m + 3) % 4, missing + 2 * ((m // 2) % 2))
    slot1 = jnp.where(diagonal, (m + 2) % 4, missing + 2 * ((m // 2 + 1) % 2))
    slots = jnp.stack([slot1, jnp.where(diagonal, slot1, r0), slot0, r0, r1]).astype(jnp.int32)
    extra = jnp.where(m < 2, extra.T, extra)
    all_tokens = tokens * NY * NZ * 2
    hessian = assemble(2.0 / all_tokens, slots, hess, mirrored[0], mirrored[1], extra)

    raw = project(depth_tiles(3), mine, other, left, raw)
    raw = project(depth_tiles(1), mine, other, right, raw)
    raw = project(depth_tiles(2), mine, other, jnp.concatenate([fl, fr], axis=0), raw)
    cosine, sine = turns(positions(token_ids))
    queries = rope(raw[0], send(raw[1], "k", 1), cosine, sine)

    def keys_of(x):
        x = lax.dynamic_slice_in_dim(x, k * half, half, 1)
        return lax.dot_general(x, wk, (((1,), (1,)), ((), ())), preferred_element_type=f32)

    at = (column * kwidth) % HEAD
    whole = lambda x: jnp.concatenate([x] * (HEAD // kwidth), axis=1)
    keys = rope(whole(keys_of(mine)), whole(send(keys_of(other), "k", 1)), cosine, sine)
    keys = lax.dynamic_slice_in_dim(keys, at, kwidth, 1)
    return (queries, keys, hessian)


def solution(mesh):
    fine = Mesh(mesh.devices.reshape(NZ, NY, 2, 4, 2), ALL)
    placed = (P(TOK, None), P(), P(TOK), P(), P(TOK, None, COL), P(TOK, None, COL))
    return jax.shard_map(
        shards,
        mesh=fine,
        in_specs=placed,
        out_specs=(P(TOK, COL), P(TOK, COL), P(COL, TOK)),
        check_vma=False,
    )
```

```python
import functools

import jax
import jax.numpy as jnp
from jax import lax
from jax.experimental import pallas as pl
from jax.experimental.pallas import tpu as pltpu
from jax.sharding import Mesh, PartitionSpec as P

HEAD = 128
SEQ = 128


begin_token = 128000
rope_base = 500000.0

NY, NZ, NC = 4, 4, 8
TOK = ("zl", "y", "k")
COL = ("x", "zh")
ALL = TOK + COL
SIZES = {"y": NY, "zl": NZ, "k": 2}
f32, bf16 = jnp.float32, jnp.bfloat16


def send(array, axis, shift):
    n = SIZES[axis]
    return lax.ppermute(array, axis, [(i, (i + shift) % n) for i in range(n)])


together = lax.optimization_barrier


def pick(array, index):
    return lax.dynamic_index_in_dim(array, index, 0, keepdims=False)


def positions(token_ids):
    samples = token_ids.reshape(-1, SEQ)
    index = jnp.arange(SEQ, dtype=jnp.int32)
    starts = jnp.where(samples == begin_token, index[None, :], 0)
    seen = index[None, :] <= index[:, None]
    latest = jnp.max(jnp.where(seen[None], starts[:, None, :], 0), axis=2)
    return (index[None, :] - latest).reshape(-1)


def turns(place):
    dims = jnp.arange(HEAD, dtype=jnp.int32)
    pair = (dims // 2).astype(f32)
    freq = jnp.power(f32(rope_base), -2.0 * pair / HEAD)
    angle = place.astype(f32)[:, None] * freq[None, :]
    sign = jnp.where(dims % 2 == 0, -1.0, 1.0).astype(f32)
    return jnp.cos(angle), jnp.sin(angle) * sign[None, :]


def normalize(hidden, norm_gain):
    wide = hidden.astype(f32)
    meansq = jnp.mean(wide * wide, axis=-1, keepdims=True)
    return (wide * lax.rsqrt(meansq + 1e-05) * norm_gain[None, :]).astype(bf16)


def across(left, right):
    return lax.dot_general(left, right, (((0,), (0,)), ((), ())), preferred_element_type=f32)


def gram_body(table, *refs):
    ca, cb, r0a, r0b, r1a, r1b = (ref[...] for ref in refs[:6])
    low, high, base = refs[6:]
    slot = pl.program_id(0)
    half = NZ // 2
    ta, tb = ca.T, cb.T
    dot = functools.partial(jnp.dot, preferred_element_type=f32)
    tile = jnp.concatenate([dot(ta, r0a) + dot(tb, r0b), dot(ta, r1a) + dot(tb, r1b)], axis=1)

    @pl.when(slot < half)
    def _():
        low[0] = tile.astype(bf16)

    @pl.when((slot >= half) & (slot < NZ))
    def _():
        high[0] = tile.astype(bf16)

    @pl.when(slot >= NZ)
    def _():
        base[0] = tile


def gram(table, mine, other):
    tokens, depth = mine.shape
    n = table.shape[1]
    tile = depth // (NY * NZ * 2)
    half = NZ // 2
    at = lambda row: pl.BlockSpec((tokens, tile), lambda s, tab: (0, tab[row, s]))
    block = (1, tile, 2 * tile)
    shape = lambda n, kind: jax.ShapeDtypeStruct((n, tile, 2 * tile), kind)
    return pl.pallas_call(
        gram_body,
        grid_spec=pltpu.PrefetchScalarGridSpec(
            num_scalar_prefetch=1,
            grid=(n,),
            in_specs=[at(0), at(0), at(1), at(1), at(2), at(2)],
            out_specs=[
                pl.BlockSpec(block, lambda s, tab: (jnp.minimum(s, half - 1), 0, 0)),
                pl.BlockSpec(block, lambda s, tab: (jnp.clip(s - half, 0, half - 1), 0, 0)),
                pl.BlockSpec(block, lambda s, tab: (jnp.maximum(s - NZ, 0), 0, 0)),
            ],
        ),
        out_shape=[shape(half, bf16), shape(half, bf16), shape(n - NZ, f32)],
        cost_estimate=pl.CostEstimate(
            flops=8 * tokens * 2 * tile * tile * n,
            bytes_accessed=8 * n * tokens * tile * 2,
            transcendentals=0,
        ),
        name="gram",
    )(table, mine, other, mine, other, mine, other)


def project_body(slots, piece, fresh, table, *refs):
    out = refs[-1]
    ma, mb = refs[:slots], refs[slots : 2 * slots]
    ws = refs[2 * slots : -1 if fresh else -2]
    width = ws[0].shape[2]
    depth_of = [(w, i) for w in ws for i in range(w.shape[0])]
    keys = []
    for w, i in depth_of:
        kt = w[i, piece:, :]
        kt = [kt[:, :piece], kt[:, piece:]]
        keys.append(jnp.concatenate(kt + kt, axis=0))
    for core, tokens in ((0, ma), (1, mb)):
        main = jnp.zeros(out.shape[1:2] + (width,), f32) if fresh else refs[-2][core, :, :width]
        side = jnp.zeros(out.shape[1:2] + (HEAD,), f32) if fresh else refs[-2][core, :, width:]
        for (w, i), x, kt in zip(depth_of, tokens, keys):
            main += jnp.dot(x[...], w[i, :piece, :], preferred_element_type=f32)
            side += lax.dot_general(
                x[...], kt, (((1,), (1,)), ((), ())), preferred_element_type=f32
            )
        out[core, :, :width] = main
        out[core, :, width:] = side


def project(table, mine, other, weights, sofar=None):
    tokens = mine.shape[0]
    slots = table.shape[0]
    rows, width = weights[0].shape[1:]
    piece = width // 2
    at = [pl.BlockSpec((tokens, piece), lambda s, tab, n=n: (0, tab[n])) for n in range(slots)]
    full = lambda shape: pl.BlockSpec(shape, lambda s, tab: (0, 0, 0))
    whole = (2, tokens, width + HEAD)
    fresh = sofar is None
    return pl.pallas_call(
        functools.partial(project_body, slots, piece, fresh),
        grid_spec=pltpu.PrefetchScalarGridSpec(
            num_scalar_prefetch=1,
            grid=(1,),
            in_specs=at + at + [full(w.shape) for w in weights] + ([] if fresh else [full(whole)]),
            out_specs=full(whole),
        ),
        out_shape=jax.ShapeDtypeStruct(whole, f32),
        cost_estimate=pl.CostEstimate(
            flops=4 * tokens * piece * width * slots,
            bytes_accessed=slots * (2 * tokens * piece + rows * width) * 2 + 16 * tokens * width,
            transcendentals=0,
        ),
        name="project",
    )(table, *[mine] * slots, *[other] * slots, *weights, *([] if fresh else [sofar]))


def rope_body(a, b, cosine, sine, queries, keys):
    even = lax.broadcasted_iota(jnp.int32, cosine.shape, 1) % 2 == 0
    width = queries.shape[1]
    for start in range(0, width + HEAD, HEAD):
        x = a[0, :, start : start + HEAD] + b[:, start : start + HEAD]
        swapped = jnp.where(even, pltpu.roll(x, HEAD - 1, 1), pltpu.roll(x, 1, 1))
        x = (x * cosine[...] + swapped * sine[...]).astype(bf16)
        if start < width:
            queries[:, start : start + HEAD] = x
        else:
            keys[...] = x


def rope(a, b, cosine, sine):
    tokens, width = b.shape
    full = lambda shape: pl.BlockSpec(shape, lambda i: (0,) * len(shape))
    shapes = [(tokens, width - HEAD), (tokens, HEAD)]
    return pl.pallas_call(
        rope_body,
        grid=(1,),
        in_specs=[full((1, tokens, width)), full(b.shape), full(cosine.shape), full(sine.shape)],
        out_specs=[full(shape) for shape in shapes],
        out_shape=[jax.ShapeDtypeStruct(shape, bf16) for shape in shapes],
        name="rope",
    )(a, b, cosine, sine)


def assemble_body(scale, slots, own, r0, r1, extra, out):
    tile = out.shape[1]

    def put(n, value):
        out[pl.ds(pl.multiple_of(slots[n] * tile, tile), tile), :] = value * scale

    put(0, r1[...].astype(f32))
    put(1, extra[...])
    put(2, r0[...].astype(f32))
    put(3, own[:, :tile].T)
    put(4, own[:, tile:].T)


def assemble(scale, slots, own, r0, r1, extra):
    tile = own.shape[0]
    return pl.pallas_call(
        functools.partial(assemble_body, scale),
        in_specs=[pl.BlockSpec(memory_space=pltpu.SMEM)] + [pl.BlockSpec(memory_space=pltpu.VMEM)] * 4,
        out_shape=jax.ShapeDtypeStruct((4 * tile, tile), f32),
        name="assemble",
    )(slots, own, r0, r1, extra)


def row_pair(t, c):
    u, m = t // 4, t % 4
    p = (t + (c > u)) % 2
    return jnp.where(c == u, m, p), jnp.where(c == u, (m + 1) % 4, p + 2)


def partner_moves(q):
    moves = []
    for t in range(NY * NZ * 2):
        for c in range(NC):
            u, m = t // 4, t % 4
            if c == u:
                r = (m + 1) % 4 if q == 0 else m
            else:
                r = (t + (c > u)) % 2 + 2 * ((q + m // 2) % 2)
            moves.append((t * NC + c, (4 * c + r) * NC + u))
    return moves


def shards(hidden, norm_gain, token_ids, owner, query_store, key_store):
    y, z, k = lax.axis_index("y"), lax.axis_index("zl"), lax.axis_index("k")
    column = lax.axis_index("x") * 2 + lax.axis_index("zh")
    root = owner[0]
    root_z, root_y, root_k = root // 8, (root // 2) % 4, root % 2

    tokens, depth = hidden.shape
    half = depth // 2
    piece = half // (NY * NZ)
    qwidth, kwidth = query_store.shape[2], key_store.shape[2]
    h = NZ // 2
    here = root_k == k

    q = query_store[0].reshape(2 * NY, 2, h * piece, qwidth)
    kt = key_store[0].T

    def stored(core, at):
        rows = pick(q, core * NY + at)
        start = (core * NY + at) * (NZ * piece)
        side = lax.dynamic_slice_in_dim(kt, start, NZ * piece, 1)
        side = jnp.stack([side[:, : h * piece], side[:, h * piece :]], axis=0)
        return jnp.concatenate([rows, side], axis=1)

    def block(rel, core, here):
        at = (y + rel) % NY
        return jnp.where(here, stored(core, at), send(stored(1 - core, at), "k", 1))

    step_y = (y - root_y) % NY
    far = block(2, k, here)
    far0, far1, later_k, later = together((far[0], far[1], k, here))
    a = send(far0, "y", 1)
    b = send(far1, "y", -1)
    up, down, own = (block(rel, later_k, later) for rel in (1, 3, 0))

    mine = normalize(hidden, norm_gain)
    mine, far0 = together((mine, far0))
    other = send(mine, "k", 1)

    up = jnp.where(step_y == 1, a[None], up)
    down = jnp.where(step_y == 3, b[None], down)
    up, down, other = together((up, down, other))
    c = send(up, "y", 1)
    d = send(down, "y", -1)

    zs = (z + jnp.arange(NZ)) % NZ
    rel = jnp.array([2, 1, 3, 0])[:, None]
    t = (zs[None] * (2 * NY) + ((y + rel) % NY) * 2 + k).reshape(-1)
    r0, r1 = row_pair(t, column)
    table = jnp.stack([t, 4 * column + r0, 4 * column + r1]).astype(jnp.int32)
    p_low, p_high, base = gram(table, mine, other)

    tile = depth // (NY * NZ * 2)
    both = [lax.dynamic_slice_in_dim(x, (4 * column + k) * tile, 3 * tile, 1) for x in (mine, other)]
    extra = sum(across(x[:, :tile], x[:, 2 * tile :]) for x in both)

    def butterfly(extra, axis, bit):
        pairs = [(i, i ^ bit) for i in range(SIZES[axis])]
        return lax.ppermute(extra.astype(bf16), axis, pairs).astype(f32)

    low = lax.broadcasted_iota(jnp.int32, (2, 1, 1), 0) == 0
    from_c = (step_y == 1) | ((step_y == 2) & low)
    quarter = jnp.where(step_y == 0, own, jnp.where(from_c, c, d))
    side = quarter[:, h * piece :].reshape(2, 2, kwidth // 2, 2, piece)
    side = side.transpose(0, 3, 2, 1, 4).reshape(NZ, kwidth // 2, 2 * piece)
    quarter = quarter[:, : h * piece].reshape(NZ, piece, qwidth)
    quarter = jnp.concatenate([quarter, side], axis=1)
    p_low, p_high, base, quarter, extra = together((p_low, p_high, base, quarter, extra))

    ga = send(p_low, "y", 1)
    gb = send(p_high, "y", -1)
    step_z = (z - root_z) % NZ
    got = [pick(quarter, z)] + [send(pick(quarter, (z + s) % NZ), "zl", s) for s in (1, 2, 3)]
    ea = butterfly(extra, "y", 1)
    first = lax.broadcasted_iota(jnp.int32, (2, 1, 1, 1), 0) == 0
    shape = (2, h, tile, 2 * tile)
    up = base[:NZ].reshape(shape) + jnp.where(first, ga.astype(f32)[None], 0.0)
    down = base[NZ : 2 * NZ].reshape(shape) + jnp.where(first, 0.0, gb.astype(f32)[None])
    up, down, step_z = together((up.astype(bf16), down.astype(bf16), step_z))
    gc = send(up, "y", 1).reshape(NZ, tile, 2 * tile)
    gd = send(down, "y", -1).reshape(NZ, tile, 2 * tile)
    extra = extra + ea
    eb = butterfly(extra, "y", 2)
    seed = got[0]
    for s in (1, 2, 3):
        seed = jnp.where(step_z == s, got[s], seed)
    strip = jnp.stack([seed] + [send(seed, "zl", -s) for s in (1, 2, 3)], axis=0)
    total = [base[2 * NZ + s] + gc[s].astype(f32) + gd[s].astype(f32) for s in range(NZ)]
    hess, rest = total[0], [x.astype(bf16) for x in total[1:]]
    extra = extra + eb
    strip, hess, rest, extra = together((strip, hess, rest, extra))

    def depth_tiles(rel):
        return (k * NY * NZ + ((y + rel) % NY) * NZ + zs).astype(jnp.int32)

    left = send(strip, "y", 1)
    right = send(strip, "y", -1)
    parts = [send(rest[s - 1], "zl", s) for s in (1, 2, 3)]
    ec = butterfly(extra, "zl", 1)
    raw = project(depth_tiles(0), mine, other, [strip])
    cosine, sine = turns(positions(token_ids))
    left, right, parts, ec, raw, cosine, sine = together((left, right, parts, ec, raw, cosine, sine))
    fl = send(left[:h], "y", 1)
    fr = send(right[h:], "y", -1)
    for part in parts:
        hess = hess + part.astype(f32)

    t = z * (2 * NY) + y * 2 + k
    u, m = t // 4, t % 4
    diagonal = column == u
    r0, r1 = row_pair(t, column)
    tiles, raw = together((hess.astype(bf16), raw))
    tiles = [tiles[:, :tile], tiles[:, tile:]]
    mirrored = []
    for n in (0, 1):
        second = jnp.where(diagonal, 1, (n + m // 2) % 2) == 1
        mirrored.append(lax.ppermute(jnp.where(second, tiles[1], tiles[0]), ALL, partner_moves(n)))
    extra = extra + ec
    extra = extra + butterfly(extra, "zl", 2)
    missing = 1 - r0 % 2
    slot0 = jnp.where(diagonal, (m + 3) % 4, missing + 2 * ((m // 2) % 2))
    slot1 = jnp.where(diagonal, (m + 2) % 4, missing + 2 * ((m // 2 + 1) % 2))
    slots = jnp.stack([slot1, jnp.where(diagonal, slot1, r0), slot0, r0, r1]).astype(jnp.int32)
    extra = jnp.where(m < 2, extra.T, extra)
    all_tokens = tokens * NY * NZ * 2
    hessian = assemble(2.0 / all_tokens, slots, hess, mirrored[0], mirrored[1], extra)

    tiles = jnp.concatenate([depth_tiles(3), depth_tiles(1)])
    raw = project(tiles, mine, other, [left, right], raw)
    raw = project(depth_tiles(2), mine, other, [fl, fr], raw)
    queries, keys = rope(raw, send(raw[1], "k", 1), cosine, sine)
    keys = lax.dynamic_slice_in_dim(keys, (column * kwidth) % HEAD, kwidth, 1)
    return (queries, keys, hessian)


def solution(mesh):
    fine = Mesh(mesh.devices.reshape(NZ, NY, 2, 4, 2), ALL)
    placed = (P(TOK, None), P(), P(TOK), P(), P(TOK, None, COL), P(TOK, None, COL))
    return jax.shard_map(
        shards,
        mesh=fine,
        in_specs=placed,
        out_specs=(P(TOK, COL), P(TOK, COL), P(COL, TOK)),
        check_vma=False,
    )
```

```python
import functools

import jax
import jax.numpy as jnp
from jax import lax
from jax.experimental import pallas as pl
from jax.experimental.pallas import tpu as pltpu
from jax.sharding import Mesh, PartitionSpec as P

HEAD = 128
SEQ = 128


begin_token = 128000
rope_base = 500000.0

NY, NZ, NC = 4, 4, 8
TOK = ("zl", "y", "k")
COL = ("x", "zh")
ALL = TOK + COL
SIZES = {"y": NY, "zl": NZ, "k": 2}
f32, bf16 = jnp.float32, jnp.bfloat16


def send(array, axis, shift):
    n = SIZES[axis]
    return lax.ppermute(array, axis, [(i, (i + shift) % n) for i in range(n)])


together = lax.optimization_barrier


def pick(array, index):
    return lax.dynamic_index_in_dim(array, index, 0, keepdims=False)


def positions(token_ids):
    samples = token_ids.reshape(-1, SEQ)
    index = jnp.arange(SEQ, dtype=jnp.int32)
    starts = jnp.where(samples == begin_token, index[None, :], 0)
    seen = index[None, :] <= index[:, None]
    latest = jnp.max(jnp.where(seen[None], starts[:, None, :], 0), axis=2)
    return (index[None, :] - latest).reshape(-1)


def turns(place):
    dims = jnp.arange(HEAD, dtype=jnp.int32)
    pair = (dims // 2).astype(f32)
    freq = jnp.power(f32(rope_base), -2.0 * pair / HEAD)
    angle = place.astype(f32)[:, None] * freq[None, :]
    sign = jnp.where(dims % 2 == 0, -1.0, 1.0).astype(f32)
    return jnp.cos(angle), jnp.sin(angle) * sign[None, :]


def row_scale(hidden):
    wide = hidden.astype(f32)
    return lax.rsqrt(jnp.mean(wide * wide, axis=-1) + 1e-05)


def normalize(hidden, scale, norm_gain):
    return (hidden.astype(f32) * scale[:, None] * norm_gain[None, :]).astype(bf16)


def across(left, right):
    return lax.dot_general(left, right, (((0,), (0,)), ((), ())), preferred_element_type=f32)


def gram_body(table, *refs):
    ca, cb, r0a, r0b, r1a, r1b = (ref[...] for ref in refs[:6])
    low, high, base = refs[6:]
    slot = pl.program_id(0)
    half = NZ // 2
    ta, tb = ca.T, cb.T
    dot = functools.partial(jnp.dot, preferred_element_type=f32)
    tile = jnp.concatenate([dot(ta, r0a) + dot(tb, r0b), dot(ta, r1a) + dot(tb, r1b)], axis=1)

    @pl.when(slot < half)
    def _():
        low[0] = tile.astype(bf16)

    @pl.when((slot >= half) & (slot < NZ))
    def _():
        high[0] = tile.astype(bf16)

    @pl.when(slot >= NZ)
    def _():
        base[0] = tile


def gram(table, mine, other):
    tokens, depth = mine.shape
    n = table.shape[1]
    tile = depth // (NY * NZ * 2)
    half = NZ // 2
    at = lambda row: pl.BlockSpec((tokens, tile), lambda s, tab: (0, tab[row, s]))
    block = (1, tile, 2 * tile)
    shape = lambda n, kind: jax.ShapeDtypeStruct((n, tile, 2 * tile), kind)
    return pl.pallas_call(
        gram_body,
        grid_spec=pltpu.PrefetchScalarGridSpec(
            num_scalar_prefetch=1,
            grid=(n,),
            in_specs=[at(0), at(0), at(1), at(1), at(2), at(2)],
            out_specs=[
                pl.BlockSpec(block, lambda s, tab: (jnp.minimum(s, half - 1), 0, 0)),
                pl.BlockSpec(block, lambda s, tab: (jnp.clip(s - half, 0, half - 1), 0, 0)),
                pl.BlockSpec(block, lambda s, tab: (jnp.maximum(s - NZ, 0), 0, 0)),
            ],
        ),
        out_shape=[shape(half, bf16), shape(half, bf16), shape(n - NZ, f32)],
        cost_estimate=pl.CostEstimate(
            flops=8 * tokens * 2 * tile * tile * n,
            bytes_accessed=8 * n * tokens * tile * 2,
            transcendentals=0,
        ),
        name="gram",
    )(table, mine, other, mine, other, mine, other)


def project_body(slots, piece, fresh, table, *refs):
    out = refs[-1]
    ma, mb = refs[:slots], refs[slots : 2 * slots]
    left, right = [], []
    for w in refs[2 * slots : -1 if fresh else -2]:
        if w.shape[2] == piece:
            side = left if len(left) == len(right) else right
            side += [w[i] for i in range(w.shape[0])]
        else:
            left += [w[i, :, :piece] for i in range(w.shape[0])]
            right += [w[i, :, piece:] for i in range(w.shape[0])]
    spans = [slice(0, piece), slice(piece, 2 * piece), slice(2 * piece, 2 * piece + HEAD)]
    for core, tokens in ((0, ma), (1, mb)):
        sums = [0.0 if fresh else refs[-2][core, :, span] for span in spans]
        for x, w0, w1 in zip(tokens, left, right):
            x = x[...]
            kt = [w0[piece:], w1[piece:]]
            kt = jnp.concatenate(kt * (HEAD // (2 * kt[0].shape[0])), axis=0)
            sums[0] += jnp.dot(x, w0[:piece], preferred_element_type=f32)
            sums[1] += jnp.dot(x, w1[:piece], preferred_element_type=f32)
            sums[2] += lax.dot_general(x, kt, (((1,), (1,)), ((), ())), preferred_element_type=f32)
        for span, value in zip(spans, sums):
            out[core, :, span] = value


def project(piece, table, mine, other, weights, sofar=None):
    tokens = mine.shape[0]
    slots = table.shape[0]
    at = [pl.BlockSpec((tokens, piece), lambda s, tab, n=n: (0, tab[n])) for n in range(slots)]
    full = lambda shape: pl.BlockSpec(shape, lambda s, tab: (0, 0, 0))
    whole = (2, tokens, 2 * piece + HEAD)
    fresh = sofar is None
    return pl.pallas_call(
        functools.partial(project_body, slots, piece, fresh),
        grid_spec=pltpu.PrefetchScalarGridSpec(
            num_scalar_prefetch=1,
            grid=(1,),
            in_specs=at + at + [full(w.shape) for w in weights] + ([] if fresh else [full(whole)]),
            out_specs=full(whole),
        ),
        out_shape=jax.ShapeDtypeStruct(whole, f32),
        cost_estimate=pl.CostEstimate(
            flops=8 * tokens * piece * piece * slots,
            bytes_accessed=slots * 8 * tokens * piece + 8 * tokens * piece,
            transcendentals=0,
        ),
        name="project",
    )(table, *[mine] * slots, *[other] * slots, *weights, *([] if fresh else [sofar]))


def rope_body(at, a, b, cosine, sine, queries, keys):
    even = lax.broadcasted_iota(jnp.int32, cosine.shape, 1) % 2 == 0
    width, part = queries.shape[1], keys.shape[0]
    for start in range(0, width + HEAD, HEAD):
        x = a[0, :, start : start + HEAD] + b[:, start : start + HEAD]
        swapped = jnp.where(even, pltpu.roll(x, HEAD - 1, 1), pltpu.roll(x, 1, 1))
        x = x * cosine[...] + swapped * sine[...]
        if start < width:
            queries[:, start : start + HEAD] = x.astype(bf16)
        else:
            x = x.T
            chosen = x[:part]
            for n in range(1, HEAD // part):
                chosen = jnp.where(at[0] == n, x[n * part : (n + 1) * part], chosen)
            keys[...] = chosen.astype(bf16)


def rope(at, part, a, b, cosine, sine):
    tokens, width = b.shape
    full = lambda shape: pl.BlockSpec(shape, lambda i: (0,) * len(shape))
    shapes = [(tokens, width - HEAD), (part, tokens)]
    return pl.pallas_call(
        rope_body,
        grid=(1,),
        in_specs=[pl.BlockSpec(memory_space=pltpu.SMEM), full((1, tokens, width))]
        + [full(x.shape) for x in (b, cosine, sine)],
        out_specs=[full(shape) for shape in shapes],
        out_shape=[jax.ShapeDtypeStruct(shape, bf16) for shape in shapes],
        name="rope",
    )(at, a, b, cosine, sine)


def assemble_body(scale, slots, own, r0, r1, extra, out):
    tile = out.shape[1]

    def put(n, value):
        out[pl.ds(pl.multiple_of(slots[n] * tile, tile), tile), :] = value * scale

    put(0, r1[...].astype(f32))
    put(1, extra[...])
    put(2, r0[...].astype(f32))
    put(3, own[:, :tile].T)
    put(4, own[:, tile:].T)


def assemble(scale, slots, own, r0, r1, extra):
    tile = own.shape[0]
    return pl.pallas_call(
        functools.partial(assemble_body, scale),
        in_specs=[pl.BlockSpec(memory_space=pltpu.SMEM)] + [pl.BlockSpec(memory_space=pltpu.VMEM)] * 4,
        out_shape=jax.ShapeDtypeStruct((4 * tile, tile), f32),
        name="assemble",
    )(slots, own, r0, r1, extra)


def row_pair(t, c):
    u, m = t // 4, t % 4
    p = (t + (c > u)) % 2
    return jnp.where(c == u, m, p), jnp.where(c == u, (m + 1) % 4, p + 2)


def partner_moves(q):
    moves = []
    for t in range(NY * NZ * 2):
        for c in range(NC):
            u, m = t // 4, t % 4
            if c == u:
                r = (m + 1) % 4 if q == 0 else m
            else:
                r = (t + (c > u)) % 2 + 2 * ((q + m // 2) % 2)
            moves.append((t * NC + c, (4 * c + r) * NC + u))
    return moves


def shards(hidden, norm_gain, token_ids, owner, query_store, key_store):
    y, z, k = lax.axis_index("y"), lax.axis_index("zl"), lax.axis_index("k")
    column = lax.axis_index("x") * 2 + lax.axis_index("zh")
    root = owner[0]
    root_z, root_y, root_k = root // 8, (root // 2) % 4, root % 2

    tokens, depth = hidden.shape
    half = depth // 2
    piece = half // (NY * NZ)
    qwidth, kwidth = query_store.shape[2], key_store.shape[2]
    h = NZ // 2
    here = root_k == k

    q = query_store[0].reshape(2 * NY, 2, h * piece, qwidth)
    kt = key_store[0].T

    def stored(core, at):
        rows = pick(q, core * NY + at)
        start = (core * NY + at) * (NZ * piece)
        side = lax.dynamic_slice_in_dim(kt, start, NZ * piece, 1)
        side = jnp.stack([side[:, : h * piece], side[:, h * piece :]], axis=0)
        return jnp.concatenate([rows, side], axis=1)

    def chip(rel):
        return (y + rel) % NY

    scale = row_scale(hidden)

    step_y = (y - root_y) % NY
    away, later_k = together((stored(1 - k, chip(2)), k))
    far = jnp.where(here, stored(k, chip(2)), send(away, "k", 1))
    others = [stored(1 - later_k, chip(rel)) for rel in (1, 3)]
    others, later_hidden, last_k = together((others, hidden, later_k))
    others = [send(x, "k", 1) for x in others]
    theirs = send(later_hidden, "k", 1)
    others.append(send(stored(1 - last_k, chip(0)), "k", 1))
    far0, far1, later = together((far[0], far[1], here))
    a = send(far0, "y", 1)
    b = send(far1, "y", -1)
    up, down, own = (
        jnp.where(later, stored(later_k, chip(rel)), x) for rel, x in zip((1, 3, 0), others)
    )
    up = jnp.where(step_y == 1, a[None], up)
    down = jnp.where(step_y == 3, b[None], down)
    up, down, gain = together((up, down, norm_gain))
    c = send(up, "y", 1)
    d = send(down, "y", -1)

    mine = normalize(hidden, scale, gain)
    other = normalize(theirs, send(scale, "k", 1), gain)

    zs = (z + jnp.arange(NZ)) % NZ

    def table(*rels):
        t = (zs[None] * (2 * NY) + chip(jnp.array(rels)[:, None]) * 2 + k).reshape(-1)
        r0, r1 = row_pair(t, column)
        return jnp.stack([t, 4 * column + r0, 4 * column + r1]).astype(jnp.int32)

    tile = depth // (NY * NZ * 2)
    both = [lax.dynamic_slice_in_dim(x, (4 * column + k) * tile, 3 * tile, 1) for x in (mine, other)]
    extra = sum(across(x[:, :tile], x[:, 2 * tile :]) for x in both)

    def butterfly(extra, axis, bit):
        pairs = [(i, i ^ bit) for i in range(SIZES[axis])]
        return extra + lax.ppermute(extra.astype(bf16), axis, pairs).astype(f32)

    extra = butterfly(butterfly(extra, "y", 1), "y", 2)
    p_low, p_high, base = gram(table(2, 1, 3, 0), mine, other)

    p_low, p_high, base, extra, step_y = together((p_low, p_high, base, extra, step_y))
    low = lax.broadcasted_iota(jnp.int32, (2, 1, 1), 0) == 0
    from_c = (step_y == 1) | ((step_y == 2) & low)
    quarter = jnp.where(step_y == 0, own, jnp.where(from_c, c, d))
    side = quarter[:, h * piece :].reshape(2, 2, kwidth // 2, 2, piece)
    side = side.transpose(0, 3, 2, 1, 4).reshape(NZ, kwidth // 2, 2 * piece)
    quarter = quarter[:, : h * piece].reshape(NZ, piece, qwidth)
    quarter = jnp.concatenate([quarter, side], axis=1)
    p_low, p_high, quarter = together((p_low, p_high, quarter))

    ga = send(p_low, "y", 1)
    gb = send(p_high, "y", -1)
    step_z = (z - root_z) % NZ
    got = [pick(quarter, z)] + [send(pick(quarter, (z + s) % NZ), "zl", s) for s in (1, 2, 3)]
    first = lax.broadcasted_iota(jnp.int32, (2, 1, 1, 1), 0) == 0
    shape = (2, h, tile, 2 * tile)
    up = base[:NZ].reshape(shape) + jnp.where(first, ga.astype(f32)[None], 0.0)
    down = base[NZ : 2 * NZ].reshape(shape) + jnp.where(first, 0.0, gb.astype(f32)[None])
    up, down, step_z = together((up.astype(bf16), down.astype(bf16), step_z))
    gc = send(up, "y", 1).reshape(NZ, tile, 2 * tile)
    gd = send(down, "y", -1).reshape(NZ, tile, 2 * tile)
    seed = got[0]
    for s in (1, 2, 3):
        seed = jnp.where(step_z == s, got[s], seed)

    columns = qwidth // 2

    def along_z(seed):
        return jnp.stack([seed] + [send(seed, "zl", -s) for s in (1, 2, 3)], axis=0)

    strip0 = along_z(seed[:, :columns])
    total = [base[2 * NZ + s] + gc[s].astype(f32) + gd[s].astype(f32) for s in range(NZ)]
    hess, rest = total[0], [x.astype(bf16) for x in total[1:]]
    strip0, seed1, hess, rest = together((strip0, seed[:, columns:], hess, rest))
    left0, right0 = send(strip0, "y", 1), send(strip0, "y", -1)
    strip1 = along_z(seed1)
    strip1, left0, right0, rest = together((strip1, left0, right0, rest))
    left1, right1 = send(strip1, "y", 1), send(strip1, "y", -1)
    parts = [send(rest[s - 1], "zl", s) for s in (1, 2, 3)]

    def depth_tiles(rel):
        return (k * NY * NZ + chip(rel) * NZ + zs).astype(jnp.int32)

    product = functools.partial(project, piece)
    raw = product(depth_tiles(0), mine, other, [strip0, strip1])
    cosine, sine = turns(positions(token_ids))
    fl = jnp.concatenate([left0[:h], left1[:h]], axis=2)
    fr = jnp.concatenate([right0[h:], right1[h:]], axis=2)
    fl, fr, raw, cosine, sine = together((fl, fr, raw, cosine, sine))
    fl, fr = send(fl, "y", 1), send(fr, "y", -1)
    raw = product(
        jnp.concatenate([depth_tiles(3), depth_tiles(1)]),
        mine,
        other,
        [left0, left1, right0, right1],
        raw,
    )

    parts, extra, raw, fl, fr = together((parts, extra, raw, fl, fr))
    for x in parts:
        hess = hess + x.astype(f32)
    extra = butterfly(butterfly(extra, "zl", 1), "zl", 2)
    t = z * (2 * NY) + y * 2 + k
    u, m = t // 4, t % 4
    diagonal = column == u
    r0, r1 = row_pair(t, column)
    tiles = hess.astype(bf16)
    tiles = [tiles[:, :tile], tiles[:, tile:]]
    mirrored = []
    for n in (0, 1):
        second = jnp.where(diagonal, 1, (n + m // 2) % 2) == 1
        mirrored.append(lax.ppermute(jnp.where(second, tiles[1], tiles[0]), ALL, partner_moves(n)))
    missing = 1 - r0 % 2
    slot0 = jnp.where(diagonal, (m + 3) % 4, missing + 2 * ((m // 2) % 2))
    slot1 = jnp.where(diagonal, (m + 2) % 4, missing + 2 * ((m // 2 + 1) % 2))
    slots = jnp.stack([slot1, jnp.where(diagonal, slot1, r0), slot0, r0, r1]).astype(jnp.int32)
    extra = jnp.where(m < 2, extra.T, extra)
    mirrored, extra, raw = together((mirrored, extra, raw))
    all_tokens = tokens * NY * NZ * 2
    hessian = assemble(2.0 / all_tokens, slots, hess, mirrored[0], mirrored[1], extra)

    raw = product(depth_tiles(2), mine, other, [fl, fr], raw)
    at = ((column * kwidth) % HEAD) // kwidth
    queries, keys = rope(at.reshape(1), kwidth, raw, send(raw[1], "k", 1), cosine, sine)
    return (queries, keys.T, hessian)


def solution(mesh):
    fine = Mesh(mesh.devices.reshape(NZ, NY, 2, 4, 2), ALL)
    placed = (P(TOK, None), P(), P(TOK), P(), P(TOK, None, COL), P(TOK, None, COL))
    return jax.shard_map(
        shards,
        mesh=fine,
        in_specs=placed,
        out_specs=(P(TOK, COL), P(TOK, COL), P(COL, TOK)),
        check_vma=False,
    )
```

```python
import functools

import jax
import jax.numpy as jnp
from jax import lax
from jax.experimental import pallas as pl
from jax.experimental.pallas import tpu as pltpu
from jax.sharding import Mesh, PartitionSpec as P

HEAD = 128
SEQ = 128


begin_token = 128000
rope_base = 500000.0

NY, NZ, NC = 4, 4, 8
TOK = ("zl", "y", "k")
COL = ("x", "zh")
ALL = TOK + COL
SIZES = {"y": NY, "zl": NZ, "k": 2}
f32, bf16 = jnp.float32, jnp.bfloat16


def send(array, axis, shift):
    n = SIZES[axis]
    return lax.ppermute(array, axis, [(i, (i + shift) % n) for i in range(n)])


def swap(array, axis, bit):
    return lax.ppermute(array, axis, [(i, i ^ bit) for i in range(SIZES[axis])])


together = lax.optimization_barrier


def pick(array, index):
    return lax.dynamic_index_in_dim(array, index, 0, keepdims=False)


def positions(token_ids):
    samples = token_ids.reshape(-1, SEQ)
    index = jnp.arange(SEQ, dtype=jnp.int32)
    starts = jnp.where(samples == begin_token, index[None, :], 0)
    seen = index[None, :] <= index[:, None]
    latest = jnp.max(jnp.where(seen[None], starts[:, None, :], 0), axis=2)
    return (index[None, :] - latest).reshape(-1)


def turns(place):
    dims = jnp.arange(HEAD, dtype=jnp.int32)
    pair = (dims // 2).astype(f32)
    freq = jnp.power(f32(rope_base), -2.0 * pair / HEAD)
    angle = place.astype(f32)[:, None] * freq[None, :]
    sign = jnp.where(dims % 2 == 0, -1.0, 1.0).astype(f32)
    return jnp.cos(angle), jnp.sin(angle) * sign[None, :]


def normalize_body(x, gain, out):
    wide = x[...].astype(f32)
    meansq = jnp.mean(wide * wide, axis=-1, keepdims=True)
    out[...] = (wide * lax.rsqrt(meansq + 1e-05) * gain[...]).astype(bf16)


def normalize(hidden, norm_gain):
    tokens, depth = hidden.shape
    rows = 32
    return pl.pallas_call(
        normalize_body,
        grid=(tokens // rows,),
        in_specs=[
            pl.BlockSpec((rows, depth), lambda i: (i, 0)),
            pl.BlockSpec((1, depth), lambda i: (0, 0)),
        ],
        out_specs=pl.BlockSpec((rows, depth), lambda i: (i, 0)),
        out_shape=jax.ShapeDtypeStruct(hidden.shape, bf16),
        cost_estimate=pl.CostEstimate(
            flops=5 * tokens * depth, bytes_accessed=4 * tokens * depth, transcendentals=tokens
        ),
        name="normalize",
    )(hidden, norm_gain.reshape(1, depth))


def block_body(role, table, q, kt, *refs):
    n = q.shape[0]
    outs = refs[-2:] if role == "far" else refs[-1:]
    p = pl.program_id(0)

    def value(span, home):
        home = home[...]
        if role == "pack":
            return home
        x = jnp.where(table[1] == 1, home, refs[0][0, span])
        if role == "relay":
            x = jnp.where(table[2] == 1, refs[1][span], x)
        if role == "quarter":
            got = jnp.where(table[3 + p] == 1, refs[1][0, span], refs[2][0, span])
            x = jnp.where(table[2] == 1, x, got)
        return x

    rows, side = value(slice(0, n), q), value(slice(n, n + kt.shape[0]), kt)
    if role == "far":
        for index, out in enumerate(outs):

            @pl.when(p == index)
            def _():
                out[:n] = rows
                out[n:] = side

    elif role == "quarter":
        piece, high = n // 2, kt.shape[0] // 2
        for i in range(2):
            span = slice(i * piece, (i + 1) * piece)
            outs[0][i, :piece] = rows[span]
            outs[0][i, piece:] = jnp.concatenate([side[:high, span], side[high:, span]], axis=1)
    else:
        outs[0][0, :n] = rows
        outs[0][0, n:] = side


def weight_block(role, table, q, kt, *more):
    width, side = q.shape[1], kt.shape[0]
    n = q.shape[0] // (4 * NY)
    rows = n + side
    pair = pl.BlockSpec((1, rows, width), lambda p, tab: (p, 0, 0))
    single = pl.BlockSpec((rows, width), lambda p, tab: (0, 0))
    ins = [
        pl.BlockSpec((n, width), lambda p, tab: (2 * tab[0] + p, 0)),
        pl.BlockSpec((side, width), lambda p, tab: (0, 2 * tab[0] + p)),
    ] + [pair if x.ndim == 3 else single for x in more]
    shape = lambda *dims: jax.ShapeDtypeStruct(dims, bf16)
    if role == "far":
        outs, shapes = [single, single], [shape(rows, width)] * 2
    elif role == "quarter":
        outs = pl.BlockSpec((2, rows // 2, width), lambda p, tab: (p, 0, 0))
        shapes = shape(4, rows // 2, width)
    else:
        outs, shapes = pair, shape(2, rows, width)
    return pl.pallas_call(
        functools.partial(block_body, role),
        grid_spec=pltpu.PrefetchScalarGridSpec(
            num_scalar_prefetch=1, grid=(2,), in_specs=ins, out_specs=outs
        ),
        out_shape=shapes,
        cost_estimate=pl.CostEstimate(
            flops=0, bytes_accessed=4 * rows * width * (2 + len(more)), transcendentals=0
        ),
        name="block_" + role,
    )(table.astype(jnp.int32), q, kt, *more)


def across(left, right):
    return lax.dot_general(left, right, (((0,), (0,)), ((), ())), preferred_element_type=f32)


def gram_body(table, *refs):
    ca, cb, r0a, r0b, r1a, r1b = (ref[...] for ref in refs[:6])
    low, high, base = refs[6:]
    slot = pl.program_id(0)
    half = NZ // 2
    ta, tb = ca.T, cb.T
    dot = functools.partial(jnp.dot, preferred_element_type=f32)
    tile = jnp.concatenate([dot(ta, r0a) + dot(tb, r0b), dot(ta, r1a) + dot(tb, r1b)], axis=1)

    @pl.when(slot < half)
    def _():
        low[0] = tile.astype(bf16)

    @pl.when((slot >= half) & (slot < NZ))
    def _():
        high[0] = tile.astype(bf16)

    @pl.when(slot >= NZ)
    def _():
        base[0] = tile


def gram(table, mine, other):
    tokens, depth = mine.shape
    n = table.shape[1]
    tile = depth // (NY * NZ * 2)
    half = NZ // 2
    at = lambda row: pl.BlockSpec((tokens, tile), lambda s, tab: (0, tab[row, s]))
    block = (1, tile, 2 * tile)
    shape = lambda n, kind: jax.ShapeDtypeStruct((n, tile, 2 * tile), kind)
    return pl.pallas_call(
        gram_body,
        grid_spec=pltpu.PrefetchScalarGridSpec(
            num_scalar_prefetch=1,
            grid=(n,),
            in_specs=[at(0), at(0), at(1), at(1), at(2), at(2)],
            out_specs=[
                pl.BlockSpec(block, lambda s, tab: (jnp.minimum(s, half - 1), 0, 0)),
                pl.BlockSpec(block, lambda s, tab: (jnp.clip(s - half, 0, half - 1), 0, 0)),
                pl.BlockSpec(block, lambda s, tab: (jnp.maximum(s - NZ, 0), 0, 0)),
            ],
        ),
        out_shape=[shape(half, bf16), shape(half, bf16), shape(n - NZ, f32)],
        cost_estimate=pl.CostEstimate(
            flops=8 * tokens * 2 * tile * tile * n,
            bytes_accessed=8 * n * tokens * tile * 2,
            transcendentals=0,
        ),
        name="gram",
    )(table, mine, other, mine, other, mine, other)


def project_body(slots, piece, fresh, table, *refs):
    out = refs[-1]
    ma, mb = refs[:slots], refs[slots : 2 * slots]
    left, right = [], []
    for w in refs[2 * slots : -1 if fresh else -2]:
        if w.shape[2] == piece:
            side = left if len(left) == len(right) else right
            side += [w[i] for i in range(w.shape[0])]
        else:
            left += [w[i, :, :piece] for i in range(w.shape[0])]
            right += [w[i, :, piece:] for i in range(w.shape[0])]
    spans = [slice(0, piece), slice(piece, 2 * piece), slice(2 * piece, 2 * piece + HEAD)]
    for core, tokens in ((0, ma), (1, mb)):
        sums = [0.0 if fresh else refs[-2][core, :, span] for span in spans]
        for x, w0, w1 in zip(tokens, left, right):
            x = x[...]
            kt = [w0[piece:], w1[piece:]]
            kt = jnp.concatenate(kt * (HEAD // (2 * kt[0].shape[0])), axis=0)
            sums[0] += jnp.dot(x, w0[:piece], preferred_element_type=f32)
            sums[1] += jnp.dot(x, w1[:piece], preferred_element_type=f32)
            sums[2] += lax.dot_general(x, kt, (((1,), (1,)), ((), ())), preferred_element_type=f32)
        for span, value in zip(spans, sums):
            out[core, :, span] = value


def project(piece, table, mine, other, weights, sofar=None):
    tokens = mine.shape[0]
    slots = table.shape[0]
    at = [pl.BlockSpec((tokens, piece), lambda s, tab, n=n: (0, tab[n])) for n in range(slots)]
    full = lambda shape: pl.BlockSpec(shape, lambda s, tab: (0, 0, 0))
    whole = (2, tokens, 2 * piece + HEAD)
    fresh = sofar is None
    return pl.pallas_call(
        functools.partial(project_body, slots, piece, fresh),
        grid_spec=pltpu.PrefetchScalarGridSpec(
            num_scalar_prefetch=1,
            grid=(1,),
            in_specs=at + at + [full(w.shape) for w in weights] + ([] if fresh else [full(whole)]),
            out_specs=full(whole),
        ),
        out_shape=jax.ShapeDtypeStruct(whole, f32),
        cost_estimate=pl.CostEstimate(
            flops=8 * tokens * piece * piece * slots,
            bytes_accessed=slots * 8 * tokens * piece + 8 * tokens * piece,
            transcendentals=0,
        ),
        name="project",
    )(table, *[mine] * slots, *[other] * slots, *weights, *([] if fresh else [sofar]))


def rope_body(at, a, b, cosine, sine, queries, keys):
    even = lax.broadcasted_iota(jnp.int32, cosine.shape, 1) % 2 == 0
    width, part = queries.shape[1], keys.shape[0]
    for start in range(0, width + HEAD, HEAD):
        x = a[0, :, start : start + HEAD] + b[:, start : start + HEAD]
        swapped = jnp.where(even, pltpu.roll(x, HEAD - 1, 1), pltpu.roll(x, 1, 1))
        x = x * cosine[...] + swapped * sine[...]
        if start < width:
            queries[:, start : start + HEAD] = x.astype(bf16)
        else:
            x = x.T
            chosen = x[:part]
            for n in range(1, HEAD // part):
                chosen = jnp.where(at[0] == n, x[n * part : (n + 1) * part], chosen)
            keys[...] = chosen.astype(bf16)


def rope(at, part, a, b, cosine, sine):
    tokens, width = b.shape
    full = lambda shape: pl.BlockSpec(shape, lambda i: (0,) * len(shape))
    shapes = [(tokens, width - HEAD), (part, tokens)]
    return pl.pallas_call(
        rope_body,
        grid=(1,),
        in_specs=[pl.BlockSpec(memory_space=pltpu.SMEM), full((1, tokens, width))]
        + [full(x.shape) for x in (b, cosine, sine)],
        out_specs=[full(shape) for shape in shapes],
        out_shape=[jax.ShapeDtypeStruct(shape, bf16) for shape in shapes],
        name="rope",
    )(at, a, b, cosine, sine)


def assemble_body(scale, slots, own, r0, r1, extra, out):
    tile = out.shape[1]

    def put(n, value):
        out[pl.ds(pl.multiple_of(slots[n] * tile, tile), tile), :] = value * scale

    put(0, r1[...].astype(f32))
    put(1, extra[...])
    put(2, r0[...].astype(f32))
    put(3, own[:, :tile].T)
    put(4, own[:, tile:].T)


def assemble(scale, slots, own, r0, r1, extra):
    tile = own.shape[0]
    return pl.pallas_call(
        functools.partial(assemble_body, scale),
        in_specs=[pl.BlockSpec(memory_space=pltpu.SMEM)] + [pl.BlockSpec(memory_space=pltpu.VMEM)] * 4,
        out_shape=jax.ShapeDtypeStruct((4 * tile, tile), f32),
        name="assemble",
    )(slots, own, r0, r1, extra)


def row_pair(t, c):
    u, m = t // 4, t % 4
    p = (t + (c > u)) % 2
    return jnp.where(c == u, m, p), jnp.where(c == u, (m + 1) % 4, p + 2)


def partner_moves(q):
    moves = []
    for t in range(NY * NZ * 2):
        for c in range(NC):
            u, m = t // 4, t % 4
            if c == u:
                r = (m + 1) % 4 if q == 0 else m
            else:
                r = (t + (c > u)) % 2 + 2 * ((q + m // 2) % 2)
            moves.append((t * NC + c, (4 * c + r) * NC + u))
    return moves


def shards(hidden, norm_gain, token_ids, owner, query_store, key_store):
    y, z, k = lax.axis_index("y"), lax.axis_index("zl"), lax.axis_index("k")
    column = lax.axis_index("x") * 2 + lax.axis_index("zh")
    root = owner[0]
    root_z, root_y, root_k = root // 8, (root // 2) % 4, root % 2

    tokens, depth = hidden.shape
    half = depth // 2
    piece = half // (NY * NZ)
    qwidth, kwidth = query_store.shape[2], key_store.shape[2]
    h = NZ // 2
    here = root_k == k

    q = query_store[0]
    kt = key_store[0].T
    one = jnp.int32(1)

    def chip(rel):
        return (y + rel) % NY

    def told(rel, *flags):
        return jnp.stack([k * NY + chip(rel), *[x * one for x in flags]])

    def pack(k, rel):
        return weight_block("pack", jnp.stack([(1 - k) * NY + chip(rel)]), q, kt)

    step_y = (y - root_y) % NY
    far0, far1 = weight_block("far", told(2, here), q, kt, send(pack(k, 2), "k", 1))
    far0, far1, later_k = together((far0, far1, k))
    a = send(far0, "y", 1)
    b = send(far1, "y", -1)
    others = [pack(later_k, rel) for rel in (1, 3)]
    others, later_hidden, last_k = together((others, hidden, later_k))
    others = [send(x, "k", 1) for x in others]
    theirs = send(later_hidden, "k", 1)
    others.append(send(pack(last_k, 0), "k", 1))
    up = weight_block("relay", told(1, here, step_y == 1), q, kt, others[0], a)
    down = weight_block("relay", told(3, here, step_y == 3), q, kt, others[1], b)
    up, down, gain = together((up, down, norm_gain))
    c = send(up, "y", 1)
    d = send(down, "y", -1)

    mine = normalize(hidden, gain)
    other = normalize(theirs, gain)

    zs = (z + jnp.arange(NZ)) % NZ
    t = (zs[None] * (2 * NY) + chip(jnp.array([2, 1, 3, 0])[:, None]) * 2 + k).reshape(-1)
    r0, r1 = row_pair(t, column)
    table = jnp.stack([t, 4 * column + r0, 4 * column + r1]).astype(jnp.int32)
    p_low, p_high, base = gram(table, mine, other)

    tile = depth // (NY * NZ * 2)
    both = [lax.dynamic_slice_in_dim(x, (4 * column + k) * tile, 3 * tile, 1) for x in (mine, other)]
    extra = sum(across(x[:, :tile], x[:, 2 * tile :]) for x in both)

    def butterfly(extra, axis, bit):
        return extra + swap(extra.astype(bf16), axis, bit).astype(f32)

    extra = butterfly(butterfly(extra, "zl", 1), "zl", 2)
    p_low, p_high, base, extra, step_y = together((p_low, p_high, base, extra, step_y))
    flags = told(0, here, step_y == 0, (step_y == 1) | (step_y == 2), step_y == 1)
    quarter = weight_block("quarter", flags, q, kt, others[2], c, d)
    p_low, p_high, quarter = together((p_low, p_high, quarter))

    ga = send(p_low, "y", 1)
    gb = send(p_high, "y", -1)
    quarter = quarter.reshape(2, h, *quarter.shape[1:])
    kept = swap(pick(quarter, 1 - z % 2), "zl", 1)
    first = lax.broadcasted_iota(jnp.int32, (2, 1, 1, 1), 0) == 0
    shape = (2, h, tile, 2 * tile)
    up = base[:NZ].reshape(shape) + jnp.where(first, ga.astype(f32)[None], 0.0)
    down = base[NZ : 2 * NZ].reshape(shape) + jnp.where(first, 0.0, gb.astype(f32)[None])
    kept = jnp.where(z == root_z, pick(quarter, z % 2), kept)
    up, down, kept = together((up.astype(bf16), down.astype(bf16), kept))
    gc = send(up, "y", 1).reshape(NZ, tile, 2 * tile)
    gd = send(down, "y", -1).reshape(NZ, tile, 2 * tile)
    kept = jnp.where(z // 2 == root_z // 2, kept, swap(kept, "zl", 2))
    total = [base[2 * NZ + s] + gc[s].astype(f32) + gd[s].astype(f32) for s in range(NZ)]
    hess, rest = total[0], [x.astype(bf16) for x in total[1:]]
    kept, hess, rest, extra = together((kept, hess, rest, extra))
    strip = jnp.concatenate([kept, swap(kept, "zl", 1)], axis=0)
    extra = butterfly(butterfly(extra, "y", 1), "y", 2)
    strip, extra, rest = together((strip, extra, rest))

    pairs = jnp.concatenate([2 * (z % 2) + jnp.arange(2), 2 * (1 - z % 2) + jnp.arange(2)])

    def depth_tiles(rel):
        return (k * NY * NZ + chip(rel) * NZ + pairs).astype(jnp.int32)

    product = functools.partial(project, piece)
    left, right = send(strip, "y", 1), send(strip, "y", -1)
    parts = [send(rest[s - 1], "zl", s) for s in (1, 2, 3)]
    raw = product(depth_tiles(0), mine, other, [strip])
    cosine, sine = turns(positions(token_ids))
    left, right, parts, raw, cosine, sine = together((left, right, parts, raw, cosine, sine))
    fl, fr = send(left[:h], "y", 1), send(right[h:], "y", -1)

    for x in parts:
        hess = hess + x.astype(f32)
    t = z * (2 * NY) + y * 2 + k
    u, m = t // 4, t % 4
    diagonal = column == u
    r0, r1 = row_pair(t, column)
    tiles = hess.astype(bf16)
    tiles = [tiles[:, :tile], tiles[:, tile:]]
    mirrored = []
    for n in (0, 1):
        second = jnp.where(diagonal, 1, (n + m // 2) % 2) == 1
        mirrored.append(lax.ppermute(jnp.where(second, tiles[1], tiles[0]), ALL, partner_moves(n)))
    missing = 1 - r0 % 2
    slot0 = jnp.where(diagonal, (m + 3) % 4, missing + 2 * ((m // 2) % 2))
    slot1 = jnp.where(diagonal, (m + 2) % 4, missing + 2 * ((m // 2 + 1) % 2))
    slots = jnp.stack([slot1, jnp.where(diagonal, slot1, r0), slot0, r0, r1]).astype(jnp.int32)
    extra = jnp.where(m < 2, extra.T, extra)

    sides = jnp.concatenate([depth_tiles(3), depth_tiles(1)])
    raw = product(sides, mine, other, [left, right], raw)
    mirrored, raw = together((mirrored, raw))
    raw = product(depth_tiles(2), mine, other, [fl, fr], raw)
    all_tokens = tokens * NY * NZ * 2
    hessian = assemble(2.0 / all_tokens, slots, hess, mirrored[0], mirrored[1], extra)
    at = ((column * kwidth) % HEAD) // kwidth
    queries, keys = rope(at.reshape(1), kwidth, raw, send(raw[1], "k", 1), cosine, sine)
    return (queries, keys.T, hessian)


def solution(mesh):
    fine = Mesh(mesh.devices.reshape(NZ, NY, 2, 4, 2), ALL)
    placed = (P(TOK, None), P(), P(TOK), P(), P(TOK, None, COL), P(TOK, None, COL))
    return jax.shard_map(
        shards,
        mesh=fine,
        in_specs=placed,
        out_specs=(P(TOK, COL), P(TOK, COL), P(COL, TOK)),
        check_vma=False,
    )
```

```python
import functools

import jax
import jax.numpy as jnp
from jax import lax
from jax.experimental import pallas as pl
from jax.experimental.pallas import tpu as pltpu
from jax.sharding import Mesh, PartitionSpec as P

HEAD = 128
SEQ = 128


begin_token = 128000
rope_base = 500000.0

NY, NZ, NC = 4, 4, 8
TOK = ("zl", "y", "k")
COL = ("x", "zh")
ALL = TOK + COL
SIZES = {"y": NY, "zl": NZ, "k": 2}
f32, bf16 = jnp.float32, jnp.bfloat16


def send(array, axis, shift):
    n = SIZES[axis]
    return lax.ppermute(array, axis, [(i, (i + shift) % n) for i in range(n)])


def swap(array, axis, bit):
    return lax.ppermute(array, axis, [(i, i ^ bit) for i in range(SIZES[axis])])


together = lax.optimization_barrier


def pick(array, index):
    return lax.dynamic_index_in_dim(array, index, 0, keepdims=False)


def positions(token_ids):
    samples = token_ids.reshape(-1, SEQ)
    index = jnp.arange(SEQ, dtype=jnp.int32)
    starts = jnp.where(samples == begin_token, index[None, :], 0)
    seen = index[None, :] <= index[:, None]
    latest = jnp.max(jnp.where(seen[None], starts[:, None, :], 0), axis=2)
    return (index[None, :] - latest).reshape(-1)


def turns(place):
    dims = jnp.arange(HEAD, dtype=jnp.int32)
    pair = (dims // 2).astype(f32)
    freq = jnp.power(f32(rope_base), -2.0 * pair / HEAD)
    angle = place.astype(f32)[:, None] * freq[None, :]
    sign = jnp.where(dims % 2 == 0, -1.0, 1.0).astype(f32)
    return jnp.cos(angle), jnp.sin(angle) * sign[None, :]


def normalize(hidden, norm_gain):
    wide = hidden.astype(f32)
    meansq = jnp.mean(wide * wide, axis=-1, keepdims=True)
    return (wide * lax.rsqrt(meansq + 1e-05) * norm_gain[None, :]).astype(bf16)


def block_body(role, table, q, kt, *refs):
    n = q.shape[0]
    outs = refs[-2:] if role == "far" else refs[-1:]
    p = pl.program_id(0)

    def value(span, home):
        home = home[...]
        if role == "pack":
            return home
        x = jnp.where(table[1] == 1, home, refs[0][0, span])
        if role == "relay":
            x = jnp.where(table[2] == 1, refs[1][span], x)
        if role == "quarter":
            got = jnp.where(table[3 + p] == 1, refs[1][0, span], refs[2][0, span])
            x = jnp.where(table[2] == 1, x, got)
        return x

    rows, side = value(slice(0, n), q), value(slice(n, n + kt.shape[0]), kt)
    if role == "far":
        for index, out in enumerate(outs):

            @pl.when(p == index)
            def _():
                out[:n] = rows
                out[n:] = side

    elif role == "quarter":
        piece, high = n // 2, kt.shape[0] // 2
        for i in range(2):
            span = slice(i * piece, (i + 1) * piece)
            outs[0][i, :piece] = rows[span]
            outs[0][i, piece:] = jnp.concatenate([side[:high, span], side[high:, span]], axis=1)
    else:
        outs[0][0, :n] = rows
        outs[0][0, n:] = side


def weight_block(role, table, q, kt, *more):
    width, side = q.shape[1], kt.shape[0]
    n = q.shape[0] // (4 * NY)
    rows = n + side
    pair = pl.BlockSpec((1, rows, width), lambda p, tab: (p, 0, 0))
    single = pl.BlockSpec((rows, width), lambda p, tab: (0, 0))
    ins = [
        pl.BlockSpec((n, width), lambda p, tab: (2 * tab[0] + p, 0)),
        pl.BlockSpec((side, width), lambda p, tab: (0, 2 * tab[0] + p)),
    ] + [pair if x.ndim == 3 else single for x in more]
    shape = lambda *dims: jax.ShapeDtypeStruct(dims, bf16)
    if role == "far":
        outs, shapes = [single, single], [shape(rows, width)] * 2
    elif role == "quarter":
        outs = pl.BlockSpec((2, rows // 2, width), lambda p, tab: (p, 0, 0))
        shapes = shape(4, rows // 2, width)
    else:
        outs, shapes = pair, shape(2, rows, width)
    return pl.pallas_call(
        functools.partial(block_body, role),
        grid_spec=pltpu.PrefetchScalarGridSpec(
            num_scalar_prefetch=1, grid=(2,), in_specs=ins, out_specs=outs
        ),
        out_shape=shapes,
        cost_estimate=pl.CostEstimate(
            flops=0, bytes_accessed=4 * rows * width * (2 + len(more)), transcendentals=0
        ),
        name="block_" + role,
    )(table.astype(jnp.int32), q, kt, *more)


def across(left, right):
    return lax.dot_general(left, right, (((0,), (0,)), ((), ())), preferred_element_type=f32)


def gram_body(table, ca, cb, ra, rb, low, high, base, turned):
    slot = pl.program_id(0)
    half = NZ // 2
    tokens, tile = ca.shape

    @pl.when(slot == 0)
    def _():
        for n in range(4):
            span = slice(n * tile, (n + 1) * tile)
            turned[n, :, :tokens] = ra[:, span].T
            turned[n, :, tokens:] = rb[:, span].T

    columns = jnp.concatenate([ca[...], cb[...]], axis=0)
    rows = [turned[table[n, slot]] for n in (1, 2)]
    tiles = [jnp.dot(x, columns, preferred_element_type=f32) for x in rows]

    @pl.when(slot < half)
    def _():
        low[0, :tile], low[0, tile:] = (x.astype(bf16) for x in tiles)

    @pl.when((slot >= half) & (slot < NZ))
    def _():
        high[0, :tile], high[0, tile:] = (x.astype(bf16) for x in tiles)

    @pl.when(slot >= NZ)
    def _():
        base[0, :tile], base[0, tile:] = tiles


def gram(table, mine, other):
    tokens, depth = mine.shape
    n = table.shape[1]
    tile = depth // (NY * NZ * 2)
    half = NZ // 2
    cols = pl.BlockSpec((tokens, tile), lambda s, tab: (0, tab[0, s]))
    rows = pl.BlockSpec((tokens, 4 * tile), lambda s, tab: (0, tab[3, 0]))
    block = (1, 2 * tile, tile)
    shape = lambda n, kind: jax.ShapeDtypeStruct((n, 2 * tile, tile), kind)
    return pl.pallas_call(
        gram_body,
        grid_spec=pltpu.PrefetchScalarGridSpec(
            num_scalar_prefetch=1,
            grid=(n,),
            in_specs=[cols, cols, rows, rows],
            out_specs=[
                pl.BlockSpec(block, lambda s, tab: (jnp.minimum(s, half - 1), 0, 0)),
                pl.BlockSpec(block, lambda s, tab: (jnp.clip(s - half, 0, half - 1), 0, 0)),
                pl.BlockSpec(block, lambda s, tab: (jnp.maximum(s - NZ, 0), 0, 0)),
            ],
            scratch_shapes=[pltpu.VMEM((4, tile, 2 * tokens), bf16)],
        ),
        out_shape=[shape(half, bf16), shape(half, bf16), shape(n - NZ, f32)],
        cost_estimate=pl.CostEstimate(
            flops=8 * tokens * 2 * tile * tile * n,
            bytes_accessed=8 * n * tokens * tile * 2,
            transcendentals=0,
        ),
        name="gram",
    )(table, mine, other, mine, other)


def project_body(slots, piece, fresh, table, *refs):
    out = refs[-1]
    ma, mb = refs[:slots], refs[slots : 2 * slots]
    left, right = [], []
    for w in refs[2 * slots : -1 if fresh else -2]:
        if w.shape[2] == piece:
            side = left if len(left) == len(right) else right
            side += [w[i] for i in range(w.shape[0])]
        else:
            left += [w[i, :, :piece] for i in range(w.shape[0])]
            right += [w[i, :, piece:] for i in range(w.shape[0])]
    spans = [slice(0, piece), slice(piece, 2 * piece), slice(2 * piece, 2 * piece + HEAD)]
    for core, tokens in ((0, ma), (1, mb)):
        sums = [0.0 if fresh else refs[-2][core, :, span] for span in spans]
        for x, w0, w1 in zip(tokens, left, right):
            x = x[...]
            kt = [w0[piece:], w1[piece:]]
            kt = jnp.concatenate(kt * (HEAD // (2 * kt[0].shape[0])), axis=0)
            sums[0] += jnp.dot(x, w0[:piece], preferred_element_type=f32)
            sums[1] += jnp.dot(x, w1[:piece], preferred_element_type=f32)
            sums[2] += lax.dot_general(x, kt, (((1,), (1,)), ((), ())), preferred_element_type=f32)
        for span, value in zip(spans, sums):
            out[core, :, span] = value


def project(piece, table, mine, other, weights, sofar=None):
    tokens = mine.shape[0]
    slots = table.shape[0]
    at = [pl.BlockSpec((tokens, piece), lambda s, tab, n=n: (0, tab[n])) for n in range(slots)]
    full = lambda shape: pl.BlockSpec(shape, lambda s, tab: (0, 0, 0))
    whole = (2, tokens, 2 * piece + HEAD)
    fresh = sofar is None
    return pl.pallas_call(
        functools.partial(project_body, slots, piece, fresh),
        grid_spec=pltpu.PrefetchScalarGridSpec(
            num_scalar_prefetch=1,
            grid=(1,),
            in_specs=at + at + [full(w.shape) for w in weights] + ([] if fresh else [full(whole)]),
            out_specs=full(whole),
        ),
        out_shape=jax.ShapeDtypeStruct(whole, f32),
        cost_estimate=pl.CostEstimate(
            flops=8 * tokens * piece * piece * slots,
            bytes_accessed=slots * 8 * tokens * piece + 8 * tokens * piece,
            transcendentals=0,
        ),
        name="project",
    )(table, *[mine] * slots, *[other] * slots, *weights, *([] if fresh else [sofar]))


def rope_body(at, a, b, cosine, sine, queries, keys):
    even = lax.broadcasted_iota(jnp.int32, cosine.shape, 1) % 2 == 0
    width, part = queries.shape[1], keys.shape[0]
    for start in range(0, width + HEAD, HEAD):
        x = a[0, :, start : start + HEAD] + b[:, start : start + HEAD]
        swapped = jnp.where(even, pltpu.roll(x, HEAD - 1, 1), pltpu.roll(x, 1, 1))
        x = x * cosine[...] + swapped * sine[...]
        if start < width:
            queries[:, start : start + HEAD] = x.astype(bf16)
        else:
            x = x.T
            chosen = x[:part]
            for n in range(1, HEAD // part):
                chosen = jnp.where(at[0] == n, x[n * part : (n + 1) * part], chosen)
            keys[...] = chosen.astype(bf16)


def rope(at, part, a, b, cosine, sine):
    tokens, width = b.shape
    full = lambda shape: pl.BlockSpec(shape, lambda i: (0,) * len(shape))
    shapes = [(tokens, width - HEAD), (part, tokens)]
    return pl.pallas_call(
        rope_body,
        grid=(1,),
        in_specs=[pl.BlockSpec(memory_space=pltpu.SMEM), full((1, tokens, width))]
        + [full(x.shape) for x in (b, cosine, sine)],
        out_specs=[full(shape) for shape in shapes],
        out_shape=[jax.ShapeDtypeStruct(shape, bf16) for shape in shapes],
        name="rope",
    )(at, a, b, cosine, sine)


def assemble_body(scale, slots, own, r0, r1, extra, out):
    tile = out.shape[1]

    def put(n, value):
        out[pl.ds(pl.multiple_of(slots[n] * tile, tile), tile), :] = value * scale

    put(0, r1[...].astype(f32).T)
    put(1, extra[...])
    put(2, r0[...].astype(f32).T)
    put(3, own[:tile])
    put(4, own[tile:])


def assemble(scale, slots, own, r0, r1, extra):
    tile = own.shape[1]
    return pl.pallas_call(
        functools.partial(assemble_body, scale),
        in_specs=[pl.BlockSpec(memory_space=pltpu.SMEM)] + [pl.BlockSpec(memory_space=pltpu.VMEM)] * 4,
        out_shape=jax.ShapeDtypeStruct((4 * tile, tile), f32),
        name="assemble",
    )(slots, own, r0, r1, extra)


def row_pair(t, c):
    u, m = t // 4, t % 4
    p = (t + (c > u)) % 2
    return jnp.where(c == u, m, p), jnp.where(c == u, (m + 1) % 4, p + 2)


def partner_moves(q):
    moves = []
    for t in range(NY * NZ * 2):
        for c in range(NC):
            u, m = t // 4, t % 4
            if c == u:
                r = (m + 1) % 4 if q == 0 else m
            else:
                r = (t + (c > u)) % 2 + 2 * ((q + m // 2) % 2)
            moves.append((t * NC + c, (4 * c + r) * NC + u))
    return moves


def shards(hidden, norm_gain, token_ids, owner, query_store, key_store):
    y, z, k = lax.axis_index("y"), lax.axis_index("zl"), lax.axis_index("k")
    column = lax.axis_index("x") * 2 + lax.axis_index("zh")
    root = owner[0]
    root_z, root_y, root_k = root // 8, (root // 2) % 4, root % 2

    tokens, depth = hidden.shape
    half = depth // 2
    piece = half // (NY * NZ)
    qwidth, kwidth = query_store.shape[2], key_store.shape[2]
    h = NZ // 2
    here = root_k == k

    q = query_store[0]
    kt = key_store[0].T
    one = jnp.int32(1)

    def chip(rel):
        return (y + rel) % NY

    def told(rel, *flags):
        return jnp.stack([k * NY + chip(rel), *[x * one for x in flags]])

    def pack(k, rel):
        return weight_block("pack", jnp.stack([(1 - k) * NY + chip(rel)]), q, kt)

    step_y = (y - root_y) % NY
    far0, far1 = weight_block("far", told(2, here), q, kt, send(pack(k, 2), "k", 1))
    far0, far1, later_k = together((far0, far1, k))
    a = send(far0, "y", 1)
    b = send(far1, "y", -1)
    others = [pack(later_k, rel) for rel in (1, 3)]
    others, later_hidden, last_k = together((others, hidden, later_k))
    others = [send(x, "k", 1) for x in others]
    theirs = send(later_hidden, "k", 1)
    others.append(send(pack(last_k, 0), "k", 1))
    up = weight_block("relay", told(1, here, step_y == 1), q, kt, others[0], a)
    down = weight_block("relay", told(3, here, step_y == 3), q, kt, others[1], b)
    up, down, gain = together((up, down, norm_gain))
    c = send(up, "y", 1)
    d = send(down, "y", -1)

    mine = normalize(hidden, gain)
    other = normalize(theirs, gain)

    zs = (z + jnp.arange(NZ)) % NZ
    t = (zs[None] * (2 * NY) + chip(jnp.array([2, 1, 3, 0])[:, None]) * 2 + k).reshape(-1)
    r0, r1 = row_pair(t, column)
    table = jnp.stack([t, r0, r1, jnp.full_like(t, column)]).astype(jnp.int32)
    p_low, p_high, base = gram(table, mine, other)

    tile = depth // (NY * NZ * 2)
    both = [lax.dynamic_slice_in_dim(x, (4 * column + k) * tile, 3 * tile, 1) for x in (mine, other)]
    extra = sum(across(x[:, :tile], x[:, 2 * tile :]) for x in both)

    def butterfly(extra, axis, bit):
        return extra + swap(extra.astype(bf16), axis, bit).astype(f32)

    extra = butterfly(butterfly(extra, "zl", 1), "zl", 2)
    p_low, p_high, base, extra, step_y = together((p_low, p_high, base, extra, step_y))
    flags = told(0, here, step_y == 0, (step_y == 1) | (step_y == 2), step_y == 1)
    quarter = weight_block("quarter", flags, q, kt, others[2], c, d)
    p_low, p_high, quarter = together((p_low, p_high, quarter))

    ga = send(p_low, "y", 1)
    gb = send(p_high, "y", -1)
    quarter = quarter.reshape(2, h, *quarter.shape[1:])
    kept = swap(pick(quarter, 1 - z % 2), "zl", 1)
    first = lax.broadcasted_iota(jnp.int32, (2, 1, 1, 1), 0) == 0
    shape = (2, h, 2 * tile, tile)
    up = base[:NZ].reshape(shape) + jnp.where(first, ga.astype(f32)[None], 0.0)
    down = base[NZ : 2 * NZ].reshape(shape) + jnp.where(first, 0.0, gb.astype(f32)[None])
    kept = jnp.where(z == root_z, pick(quarter, z % 2), kept)
    extra = butterfly(extra, "y", 1)
    up, down, kept, extra = together((up.astype(bf16), down.astype(bf16), kept, extra))
    gc = send(up, "y", 1).reshape(NZ, 2 * tile, tile)
    gd = send(down, "y", -1).reshape(NZ, 2 * tile, tile)
    kept = jnp.where(z // 2 == root_z // 2, kept, swap(kept, "zl", 2))
    extra = butterfly(extra, "y", 2)
    total = [base[2 * NZ + s] + gc[s].astype(f32) + gd[s].astype(f32) for s in range(NZ)]
    hess, rest = total[0], [x.astype(bf16) for x in total[1:]]
    kept, hess, rest, extra = together((kept, hess, rest, extra))

    pairs = jnp.concatenate([2 * (z % 2) + jnp.arange(2), 2 * (1 - z % 2) + jnp.arange(2)])

    def depth_tiles(rel):
        return (k * NY * NZ + chip(rel) * NZ + pairs).astype(jnp.int32)

    product = functools.partial(project, piece)
    crossed = swap(kept, "zl", 1)
    left0, right0 = send(kept, "y", 1), send(kept, "y", -1)
    cosine, sine = turns(positions(token_ids))
    crossed, left0, right0, rest, cosine, sine = together(
        (crossed, left0, right0, rest, cosine, sine)
    )
    left1, right1 = send(crossed, "y", 1), send(crossed, "y", -1)
    parts = [send(rest[1], "zl", 2)]
    raw = product(depth_tiles(0), mine, other, [kept, crossed])
    left0, left1, right1, parts, raw, rest = together((left0, left1, right1, parts, raw, rest))
    fl, fr = send(left0, "y", 1), send(right1, "y", -1)
    parts += [send(rest[0], "zl", 1), send(rest[2], "zl", 3)]
    sides = jnp.concatenate([depth_tiles(3), depth_tiles(1)])
    raw = product(sides, mine, other, [left0, left1, right0, right1], raw)
    fl, fr, parts, raw = together((fl, fr, parts, raw))

    for x in parts:
        hess = hess + x.astype(f32)
    t = z * (2 * NY) + y * 2 + k
    u, m = t // 4, t % 4
    diagonal = column == u
    r0, r1 = row_pair(t, column)
    tiles, raw = together((hess.astype(bf16), raw))
    tiles = [tiles[:tile], tiles[tile:]]
    mirrored = []
    for n in (0, 1):
        second = jnp.where(diagonal, 1, (n + m // 2) % 2) == 1
        mirrored.append(lax.ppermute(jnp.where(second, tiles[1], tiles[0]), ALL, partner_moves(n)))
    missing = 1 - r0 % 2
    slot0 = jnp.where(diagonal, (m + 3) % 4, missing + 2 * ((m // 2) % 2))
    slot1 = jnp.where(diagonal, (m + 2) % 4, missing + 2 * ((m // 2 + 1) % 2))
    slots = jnp.stack([slot1, jnp.where(diagonal, slot1, r0), slot0, r0, r1]).astype(jnp.int32)
    extra = jnp.where(m < 2, extra.T, extra)

    raw = product(depth_tiles(2), mine, other, [fl, fr], raw)
    all_tokens = tokens * NY * NZ * 2
    hessian = assemble(2.0 / all_tokens, slots, hess, mirrored[0], mirrored[1], extra)
    at = ((column * kwidth) % HEAD) // kwidth
    queries, keys = rope(at.reshape(1), kwidth, raw, send(raw[1], "k", 1), cosine, sine)
    return (queries, keys.T, hessian)


def solution(mesh):
    fine = Mesh(mesh.devices.reshape(NZ, NY, 2, 4, 2), ALL)
    placed = (P(TOK, None), P(), P(TOK), P(), P(TOK, None, COL), P(TOK, None, COL))
    return jax.shard_map(
        shards,
        mesh=fine,
        in_specs=placed,
        out_specs=(P(TOK, COL), P(TOK, COL), P(COL, TOK)),
        check_vma=False,
    )
```

```python
import functools

import jax
import jax.numpy as jnp
from jax import lax
from jax.experimental import pallas as pl
from jax.experimental.pallas import tpu as pltpu
from jax.sharding import Mesh, PartitionSpec as P

HEAD = 128
SEQ = 128


begin_token = 128000
rope_base = 500000.0

NY, NZ, NC = 4, 4, 8
TOK = ("zl", "y", "k")
COL = ("x", "zh")
ALL = TOK + COL
SIZES = {"y": NY, "zl": NZ, "k": 2}
f32, bf16 = jnp.float32, jnp.bfloat16


def send(array, axis, shift):
    n = SIZES[axis]
    return lax.ppermute(array, axis, [(i, (i + shift) % n) for i in range(n)])


def swap(array, axis, bit):
    return lax.ppermute(array, axis, [(i, i ^ bit) for i in range(SIZES[axis])])


together = lax.optimization_barrier


def pick(array, index):
    return lax.dynamic_index_in_dim(array, index, 0, keepdims=False)


def positions(token_ids):
    samples = token_ids.reshape(-1, SEQ)
    index = jnp.arange(SEQ, dtype=jnp.int32)
    starts = jnp.where(samples == begin_token, index[None, :], 0)
    seen = index[None, :] <= index[:, None]
    latest = jnp.max(jnp.where(seen[None], starts[:, None, :], 0), axis=2)
    return (index[None, :] - latest).reshape(-1)


def turns(place):
    dims = jnp.arange(HEAD, dtype=jnp.int32)
    pair = (dims // 2).astype(f32)
    freq = jnp.power(f32(rope_base), -2.0 * pair / HEAD)
    angle = place.astype(f32)[:, None] * freq[None, :]
    sign = jnp.where(dims % 2 == 0, -1.0, 1.0).astype(f32)
    return jnp.cos(angle), jnp.sin(angle) * sign[None, :]


def normalize(hidden, norm_gain):
    wide = hidden.astype(f32)
    meansq = jnp.mean(wide * wide, axis=-1, keepdims=True)
    return (wide * lax.rsqrt(meansq + 1e-05) * norm_gain[None, :]).astype(bf16)


def block_body(role, table, q, kt, *refs):
    side = kt.shape[0]
    width = q.shape[1]
    n = q.shape[0] // (4 * NY)
    piece, high = n // 2, side // 2
    if role == "quarter":
        there, c, d, out, found, turned, sems = refs
    elif role == "far":
        there, *outs, sems = refs
    elif role == "relay":
        there, relay, out, sems = refs
    else:
        out, sems = refs
    if role in ("pack", "relay"):
        outs = [out.at[0], out.at[1]]

    def home(p):
        at = 2 * table[0] + p
        rows = q.at[pl.ds(pl.multiple_of(at * n, n), n), :]
        return rows, kt.at[:, pl.ds(pl.multiple_of(at * width, width), width)]

    def received(x, p):
        return x.at[p, pl.ds(0, n), :], x.at[p, pl.ds(n, side), :]

    def run(pairs):
        copies = [pltpu.make_async_copy(a, b, sems.at[i]) for i, (a, b) in enumerate(pairs)]
        for copy in copies:
            copy.start()
        for copy in copies:
            copy.wait()

    def put(p, source):
        rows, keys = source
        if role == "quarter":
            pairs = [
                (rows.at[pl.ds(i * piece, piece), :], out.at[2 * p + i, pl.ds(0, piece), :])
                for i in range(2)
            ]
            return pairs + [(keys, found.at[p])]
        to = outs[p]
        return [(rows, to.at[pl.ds(0, n), :]), (keys, to.at[pl.ds(n, side), :])]

    def choose(cases):
        left = True
        for when, pairs in cases:
            pl.when(when & left)(functools.partial(run, pairs))
            left = left & ~when

    yes = table[0] >= 0
    if role == "pack":
        run(put(0, home(0)) + put(1, home(1)))
    elif role in ("far", "relay"):
        cases = [
            (table[1] == 1, put(0, home(0)) + put(1, home(1))),
            (yes, [(there.at[p], outs[p]) for p in range(2)]),
        ]
        if role == "relay":
            cases = [(table[2] == 1, [(relay, outs[p]) for p in range(2)])] + cases
        choose(cases)
    else:
        for p in range(2):
            mine = table[2] == 1
            choose(
                [
                    (mine & (table[1] == 1), put(p, home(p))),
                    (mine, put(p, received(there, p))),
                    (table[3 + p] == 1, put(p, received(c, p))),
                    (yes, put(p, received(d, p))),
                ]
            )
        for p in range(2):
            for i in range(2):
                span = slice(i * piece, (i + 1) * piece)
                turned[2 * p + i] = jnp.concatenate(
                    [found[p, :high, span], found[p, high:, span]], axis=1
                )
        run([(turned.at[i], out.at[i, pl.ds(piece, high), :]) for i in range(4)])


def weight_block(role, table, q, kt, *more):
    width, side = q.shape[1], kt.shape[0]
    rows = q.shape[0] // (4 * NY) + side
    shape = lambda *dims: jax.ShapeDtypeStruct(dims, bf16)
    shapes = {"far": [shape(rows, width)] * 2, "quarter": [shape(4, rows // 2, width)]}
    shapes = shapes.get(role, [shape(2, rows, width)])
    scratch = [pltpu.SemaphoreType.DMA((4,))]
    if role == "quarter":
        scratch = [
            pltpu.VMEM((2, side, width), bf16),
            pltpu.VMEM((4, side // 2, width), bf16),
        ] + scratch
    anywhere = pl.BlockSpec(memory_space=pl.ANY)
    out = pl.pallas_call(
        functools.partial(block_body, role),
        grid_spec=pltpu.PrefetchScalarGridSpec(
            num_scalar_prefetch=1,
            grid=(1,),
            in_specs=[anywhere] * (2 + len(more)),
            out_specs=[anywhere] * len(shapes),
            scratch_shapes=scratch,
        ),
        out_shape=shapes,
        cost_estimate=pl.CostEstimate(
            flops=0, bytes_accessed=8 * rows * width, transcendentals=0
        ),
        name="block_" + role,
    )(table.astype(jnp.int32), q, kt, *more)
    return out if role == "far" else out[0]


def across(left, right):
    return lax.dot_general(left, right, (((0,), (0,)), ((), ())), preferred_element_type=f32)


def gram_body(table, *refs):
    cas, cbs = refs[:NZ], refs[NZ : 2 * NZ]
    ra, rb, low, high, base, turned = refs[2 * NZ :]
    group = pl.program_id(0)
    half = NZ // 2
    tokens, tile = cas[0].shape

    @pl.when(group == 0)
    def _():
        for n in range(4):
            span = slice(n * tile, (n + 1) * tile)
            turned[n, :, :tokens] = ra[:, span].T
            turned[n, :, tokens:] = rb[:, span].T

    for n in range(NZ):
        columns = jnp.concatenate([cas[n][...], cbs[n][...]], axis=0)
        rows = [turned[table[i, NZ * group + n]] for i in (1, 2)]
        tiles = [jnp.dot(x, columns, preferred_element_type=f32) for x in rows]
        far, at = (low, n) if n < half else (high, n - half)

        @pl.when(group == 0)
        def _(far=far, at=at, tiles=tiles):
            far[at, :tile], far[at, tile:] = (x.astype(bf16) for x in tiles)

        @pl.when(group > 0)
        def _(n=n, tiles=tiles):
            base[n, :tile], base[n, tile:] = tiles


def gram(table, mine, other):
    tokens, depth = mine.shape
    n = table.shape[1]
    tile = depth // (NY * NZ * 2)
    half = NZ // 2
    cols = [
        pl.BlockSpec((tokens, tile), lambda s, tab, i=i: (0, tab[0, NZ * s + i])) for i in range(NZ)
    ]
    rows = pl.BlockSpec((tokens, 4 * tile), lambda s, tab: (0, tab[3, 0]))
    fixed = pl.BlockSpec((half, 2 * tile, tile), lambda s, tab: (0, 0, 0))
    moving = pl.BlockSpec((NZ, 2 * tile, tile), lambda s, tab: (jnp.maximum(s - 1, 0), 0, 0))
    shape = lambda n, kind: jax.ShapeDtypeStruct((n, 2 * tile, tile), kind)
    return pl.pallas_call(
        gram_body,
        grid_spec=pltpu.PrefetchScalarGridSpec(
            num_scalar_prefetch=1,
            grid=(n // NZ,),
            in_specs=cols + cols + [rows, rows],
            out_specs=[fixed, fixed, moving],
            scratch_shapes=[pltpu.VMEM((4, tile, 2 * tokens), bf16)],
        ),
        out_shape=[shape(half, bf16), shape(half, bf16), shape(n - NZ, f32)],
        cost_estimate=pl.CostEstimate(
            flops=8 * tokens * 2 * tile * tile * n,
            bytes_accessed=8 * n * tokens * tile * 2,
            transcendentals=0,
        ),
        name="gram",
    )(table, *[mine] * NZ, *[other] * NZ, mine, other)


def project_body(slots, piece, fresh, table, *refs):
    out = refs[-1]
    ma, mb = refs[:slots], refs[slots : 2 * slots]
    left, right = [], []
    for w in refs[2 * slots : -1 if fresh else -2]:
        if w.shape[2] == piece:
            side = left if len(left) == len(right) else right
            side += [w[i] for i in range(w.shape[0])]
        else:
            left += [w[i, :, :piece] for i in range(w.shape[0])]
            right += [w[i, :, piece:] for i in range(w.shape[0])]
    spans = [slice(0, piece), slice(piece, 2 * piece), slice(2 * piece, 2 * piece + HEAD)]
    for core, tokens in ((0, ma), (1, mb)):
        sums = [0.0 if fresh else refs[-2][core, :, span] for span in spans]
        for x, w0, w1 in zip(tokens, left, right):
            x = x[...]
            kt = [w0[piece:], w1[piece:]]
            kt = jnp.concatenate(kt * (HEAD // (2 * kt[0].shape[0])), axis=0)
            sums[0] += jnp.dot(x, w0[:piece], preferred_element_type=f32)
            sums[1] += jnp.dot(x, w1[:piece], preferred_element_type=f32)
            sums[2] += lax.dot_general(x, kt, (((1,), (1,)), ((), ())), preferred_element_type=f32)
        for span, value in zip(spans, sums):
            out[core, :, span] = value


def project(piece, table, mine, other, weights, sofar=None):
    tokens = mine.shape[0]
    slots = table.shape[0]
    at = [pl.BlockSpec((tokens, piece), lambda s, tab, n=n: (0, tab[n])) for n in range(slots)]
    full = lambda shape: pl.BlockSpec(shape, lambda s, tab: (0, 0, 0))
    whole = (2, tokens, 2 * piece + HEAD)
    fresh = sofar is None
    return pl.pallas_call(
        functools.partial(project_body, slots, piece, fresh),
        grid_spec=pltpu.PrefetchScalarGridSpec(
            num_scalar_prefetch=1,
            grid=(1,),
            in_specs=at + at + [full(w.shape) for w in weights] + ([] if fresh else [full(whole)]),
            out_specs=full(whole),
        ),
        out_shape=jax.ShapeDtypeStruct(whole, f32),
        cost_estimate=pl.CostEstimate(
            flops=8 * tokens * piece * piece * slots,
            bytes_accessed=slots * 8 * tokens * piece + 8 * tokens * piece,
            transcendentals=0,
        ),
        name="project",
    )(table, *[mine] * slots, *[other] * slots, *weights, *([] if fresh else [sofar]))


def rope_body(at, a, b, cosine, sine, queries, keys):
    even = lax.broadcasted_iota(jnp.int32, cosine.shape, 1) % 2 == 0
    width, part = queries.shape[1], keys.shape[0]
    for start in range(0, width + HEAD, HEAD):
        x = a[0, :, start : start + HEAD] + b[:, start : start + HEAD]
        swapped = jnp.where(even, pltpu.roll(x, HEAD - 1, 1), pltpu.roll(x, 1, 1))
        x = x * cosine[...] + swapped * sine[...]
        if start < width:
            queries[:, start : start + HEAD] = x.astype(bf16)
        else:
            x = x.T
            chosen = x[:part]
            for n in range(1, HEAD // part):
                chosen = jnp.where(at[0] == n, x[n * part : (n + 1) * part], chosen)
            keys[...] = chosen.astype(bf16)


def rope(at, part, a, b, cosine, sine):
    tokens, width = b.shape
    full = lambda shape: pl.BlockSpec(shape, lambda i: (0,) * len(shape))
    shapes = [(tokens, width - HEAD), (part, tokens)]
    return pl.pallas_call(
        rope_body,
        grid=(1,),
        in_specs=[pl.BlockSpec(memory_space=pltpu.SMEM), full((1, tokens, width))]
        + [full(x.shape) for x in (b, cosine, sine)],
        out_specs=[full(shape) for shape in shapes],
        out_shape=[jax.ShapeDtypeStruct(shape, bf16) for shape in shapes],
        compiler_params=pltpu.CompilerParams(vmem_limit_bytes=12 * 2**20),
        name="rope",
    )(at, a, b, cosine, sine)


def assemble_body(scale, slots, own, r0, r1, extra, out):
    tile = out.shape[1]

    def put(n, value):
        out[pl.ds(pl.multiple_of(slots[n] * tile, tile), tile), :] = value * scale

    put(0, r1[...].astype(f32).T)
    put(1, extra[...])
    put(2, r0[...].astype(f32).T)
    put(3, own[:tile])
    put(4, own[tile:])


def assemble(scale, slots, own, r0, r1, extra):
    tile = own.shape[1]
    return pl.pallas_call(
        functools.partial(assemble_body, scale),
        in_specs=[pl.BlockSpec(memory_space=pltpu.SMEM)] + [pl.BlockSpec(memory_space=pltpu.VMEM)] * 4,
        out_shape=jax.ShapeDtypeStruct((4 * tile, tile), f32),
        compiler_params=pltpu.CompilerParams(vmem_limit_bytes=12 * 2**20),
        name="assemble",
    )(slots, own, r0, r1, extra)


def row_pair(t, c):
    u, m = t // 4, t % 4
    p = (t + (c > u)) % 2
    return jnp.where(c == u, m, p), jnp.where(c == u, (m + 1) % 4, p + 2)


def partner_moves(q):
    moves = []
    for t in range(NY * NZ * 2):
        for c in range(NC):
            u, m = t // 4, t % 4
            if c == u:
                r = (m + 1) % 4 if q == 0 else m
            else:
                r = (t + (c > u)) % 2 + 2 * ((q + m // 2) % 2)
            moves.append((t * NC + c, (4 * c + r) * NC + u))
    return moves


def shards(hidden, norm_gain, token_ids, owner, query_store, key_store):
    y, z, k = lax.axis_index("y"), lax.axis_index("zl"), lax.axis_index("k")
    column = lax.axis_index("x") * 2 + lax.axis_index("zh")
    root = owner[0]
    root_z, root_y, root_k = root // 8, (root // 2) % 4, root % 2

    tokens, depth = hidden.shape
    half = depth // 2
    piece = half // (NY * NZ)
    qwidth, kwidth = query_store.shape[2], key_store.shape[2]
    h = NZ // 2
    here = root_k == k

    q = query_store[0]
    kt = key_store[0].T
    one = jnp.int32(1)

    def chip(rel):
        return (y + rel) % NY

    def told(rel, *flags):
        return jnp.stack([k * NY + chip(rel), *[x * one for x in flags]])

    def pack(k, rel):
        return weight_block("pack", jnp.stack([(1 - k) * NY + chip(rel)]), q, kt)

    step_y = (y - root_y) % NY
    far0, far1 = weight_block("far", told(2, here), q, kt, send(pack(k, 2), "k", 1))
    far0, far1, later_k = together((far0, far1, k))
    a = send(far0, "y", 1)
    b = send(far1, "y", -1)
    others = [pack(later_k, rel) for rel in (1, 3)]
    others, later_hidden, last_k = together((others, hidden, later_k))
    others = [send(x, "k", 1) for x in others]
    theirs = send(later_hidden, "k", 1)
    others.append(send(pack(last_k, 0), "k", 1))
    up = weight_block("relay", told(1, here, step_y == 1), q, kt, others[0], a)
    down = weight_block("relay", told(3, here, step_y == 3), q, kt, others[1], b)
    up, down, gain, ours = together((up, down, norm_gain, hidden))
    c = send(up, "y", 1)
    d = send(down, "y", -1)

    mine = normalize(ours, gain)
    other = normalize(theirs, gain)

    zs = (z + jnp.arange(NZ)) % NZ
    t = (zs[None] * (2 * NY) + chip(jnp.array([2, 1, 3, 0])[:, None]) * 2 + k).reshape(-1)
    r0, r1 = row_pair(t, column)
    table = jnp.stack([t, r0, r1, jnp.full_like(t, column)]).astype(jnp.int32)
    p_low, p_high, base = gram(table, mine, other)

    tile = depth // (NY * NZ * 2)
    both = [lax.dynamic_slice_in_dim(x, (4 * column + k) * tile, 3 * tile, 1) for x in (mine, other)]
    extra = sum(across(x[:, :tile], x[:, 2 * tile :]) for x in both)

    def butterfly(extra, axis, bit):
        return extra + swap(extra.astype(bf16), axis, bit).astype(f32)

    extra = butterfly(butterfly(extra, "zl", 1), "zl", 2)
    p_low, p_high, base, extra, step_y = together((p_low, p_high, base, extra, step_y))
    flags = told(0, here, step_y == 0, (step_y == 1) | (step_y == 2), step_y == 1)
    quarter = weight_block("quarter", flags, q, kt, others[2], c, d)
    p_low, p_high, quarter = together((p_low, p_high, quarter))

    ga = send(p_low, "y", 1)
    gb = send(p_high, "y", -1)
    quarter = quarter.reshape(2, h, *quarter.shape[1:])
    kept = swap(pick(quarter, 1 - z % 2), "zl", 1)
    first = lax.broadcasted_iota(jnp.int32, (2, 1, 1, 1), 0) == 0
    shape = (2, h, 2 * tile, tile)
    up = base[:NZ].reshape(shape) + jnp.where(first, ga.astype(f32)[None], 0.0)
    down = base[NZ : 2 * NZ].reshape(shape) + jnp.where(first, 0.0, gb.astype(f32)[None])
    kept = jnp.where(z == root_z, pick(quarter, z % 2), kept)
    extra = butterfly(extra, "y", 1)
    up, down, kept, extra = together((up.astype(bf16), down.astype(bf16), kept, extra))
    gc = send(up, "y", 1).reshape(NZ, 2 * tile, tile)
    gd = send(down, "y", -1).reshape(NZ, 2 * tile, tile)
    kept = jnp.where(z // 2 == root_z // 2, kept, swap(kept, "zl", 2))
    extra = butterfly(extra, "y", 2)
    total = [base[2 * NZ + s] + gc[s].astype(f32) + gd[s].astype(f32) for s in range(NZ)]
    hess, rest = total[0], [x.astype(bf16) for x in total[1:]]
    kept, hess, rest, extra = together((kept, hess, rest, extra))

    pairs = jnp.concatenate([2 * (z % 2) + jnp.arange(2), 2 * (1 - z % 2) + jnp.arange(2)])

    def depth_tiles(rel):
        return (k * NY * NZ + chip(rel) * NZ + pairs).astype(jnp.int32)

    product = functools.partial(project, piece)
    crossed = swap(kept, "zl", 1)
    left0, right0 = send(kept, "y", 1), send(kept, "y", -1)
    cosine, sine = turns(positions(token_ids))
    crossed, left0, right0, rest, cosine, sine = together(
        (crossed, left0, right0, rest, cosine, sine)
    )
    left1, right1 = send(crossed, "y", 1), send(crossed, "y", -1)
    parts = [send(rest[1], "zl", 2)]
    raw = product(depth_tiles(0), mine, other, [kept, crossed])
    left0, left1, right1, parts, raw, rest = together((left0, left1, right1, parts, raw, rest))
    fl, fr = send(left0, "y", 1), send(right1, "y", -1)
    parts += [send(rest[0], "zl", 1), send(rest[2], "zl", 3)]
    sides = jnp.concatenate([depth_tiles(3), depth_tiles(1)])
    raw = product(sides, mine, other, [left0, left1, right0, right1], raw)
    fl, fr, parts, raw = together((fl, fr, parts, raw))

    for x in parts:
        hess = hess + x.astype(f32)
    t = z * (2 * NY) + y * 2 + k
    u, m = t // 4, t % 4
    diagonal = column == u
    r0, r1 = row_pair(t, column)
    tiles, raw = together((hess.astype(bf16), raw))
    tiles = [tiles[:tile], tiles[tile:]]
    mirrored = []
    for n in (0, 1):
        second = jnp.where(diagonal, 1, (n + m // 2) % 2) == 1
        mirrored.append(lax.ppermute(jnp.where(second, tiles[1], tiles[0]), ALL, partner_moves(n)))
    missing = 1 - r0 % 2
    slot0 = jnp.where(diagonal, (m + 3) % 4, missing + 2 * ((m // 2) % 2))
    slot1 = jnp.where(diagonal, (m + 2) % 4, missing + 2 * ((m // 2 + 1) % 2))
    slots = jnp.stack([slot1, jnp.where(diagonal, slot1, r0), slot0, r0, r1]).astype(jnp.int32)
    extra = jnp.where(m < 2, extra.T, extra)

    raw = product(depth_tiles(2), mine, other, [fl, fr], raw)
    all_tokens = tokens * NY * NZ * 2
    hessian = assemble(2.0 / all_tokens, slots, hess, mirrored[0], mirrored[1], extra)
    at = ((column * kwidth) % HEAD) // kwidth
    queries, keys = rope(at.reshape(1), kwidth, raw, send(raw[1], "k", 1), cosine, sine)
    return (queries, keys.T, hessian)


def solution(mesh):
    fine = Mesh(mesh.devices.reshape(NZ, NY, 2, 4, 2), ALL)
    placed = (P(TOK, None), P(), P(TOK), P(), P(TOK, None, COL), P(TOK, None, COL))
    return jax.shard_map(
        shards,
        mesh=fine,
        in_specs=placed,
        out_specs=(P(TOK, COL), P(TOK, COL), P(COL, TOK)),
        check_vma=False,
    )
```

```python
import functools

import jax
import jax.numpy as jnp
from jax import lax
from jax.experimental import pallas as pl
from jax.experimental.pallas import tpu as pltpu
from jax.sharding import Mesh, PartitionSpec as P

HEAD = 128
SEQ = 128


begin_token = 128000
rope_base = 500000.0

NY, NZ, NC = 4, 4, 8
TOK = ("zl", "y", "k")
COL = ("x", "zh")
ALL = TOK + COL
SIZES = {"y": NY, "zl": NZ, "k": 2}
f32, bf16 = jnp.float32, jnp.bfloat16


def send(array, axis, shift):
    n = SIZES[axis]
    return lax.ppermute(array, axis, [(i, (i + shift) % n) for i in range(n)])


def swap(array, axis, bit):
    return lax.ppermute(array, axis, [(i, i ^ bit) for i in range(SIZES[axis])])


together = lax.optimization_barrier


def pick(array, index):
    return lax.dynamic_index_in_dim(array, index, 0, keepdims=False)


def positions(token_ids):
    samples = token_ids.reshape(-1, SEQ)
    index = jnp.arange(SEQ, dtype=jnp.int32)
    starts = jnp.where(samples == begin_token, index[None, :], 0)
    seen = index[None, :] <= index[:, None]
    latest = jnp.max(jnp.where(seen[None], starts[:, None, :], 0), axis=2)
    return (index[None, :] - latest).reshape(-1)


def turns(place):
    dims = jnp.arange(HEAD, dtype=jnp.int32)
    pair = (dims // 2).astype(f32)
    freq = jnp.power(f32(rope_base), -2.0 * pair / HEAD)
    angle = place.astype(f32)[:, None] * freq[None, :]
    sign = jnp.where(dims % 2 == 0, -1.0, 1.0).astype(f32)
    return jnp.cos(angle), jnp.sin(angle) * sign[None, :]


def normalize(hidden, norm_gain):
    wide = hidden.astype(f32)
    meansq = jnp.mean(wide * wide, axis=-1, keepdims=True)
    return (wide * lax.rsqrt(meansq + 1e-05) * norm_gain[None, :]).astype(bf16)


def pack_body(table, q, kt, out):
    n = q.shape[0]
    out[0, :n] = q[...]
    out[0, n:] = kt[...]


def pack(at, q, kt):
    width, side = q.shape[1], kt.shape[0]
    n = q.shape[0] // (4 * NY)
    return pl.pallas_call(
        pack_body,
        grid_spec=pltpu.PrefetchScalarGridSpec(
            num_scalar_prefetch=1,
            grid=(2,),
            in_specs=[
                pl.BlockSpec((n, width), lambda p, tab: (2 * tab[0] + p, 0)),
                pl.BlockSpec((side, width), lambda p, tab: (0, 2 * tab[0] + p)),
            ],
            out_specs=pl.BlockSpec((1, n + side, width), lambda p, tab: (p, 0, 0)),
        ),
        out_shape=jax.ShapeDtypeStruct((2, n + side, width), bf16),
        cost_estimate=pl.CostEstimate(
            flops=0, bytes_accessed=8 * (n + side) * width, transcendentals=0
        ),
        name="pack",
    )(at.reshape(1).astype(jnp.int32), q, kt)


def across(left, right):
    return lax.dot_general(left, right, (((0,), (0,)), ((), ())), preferred_element_type=f32)


def gram_body(table, *refs):
    cas, cbs = refs[:NZ], refs[NZ : 2 * NZ]
    ra, rb, low, high, base, turned = refs[2 * NZ :]
    group = pl.program_id(0)
    half = NZ // 2
    tokens, tile = cas[0].shape

    @pl.when(group == 0)
    def _():
        for n in range(4):
            span = slice(n * tile, (n + 1) * tile)
            turned[n, :, :tokens] = ra[:, span].T
            turned[n, :, tokens:] = rb[:, span].T

    for n in range(NZ):
        columns = jnp.concatenate([cas[n][...], cbs[n][...]], axis=0)
        rows = [turned[table[i, NZ * group + n]] for i in (1, 2)]
        tiles = [jnp.dot(x, columns, preferred_element_type=f32) for x in rows]
        far, at = (low, n) if n < half else (high, n - half)

        @pl.when(group == 0)
        def _(far=far, at=at, tiles=tiles):
            far[at, :tile], far[at, tile:] = (x.astype(bf16) for x in tiles)

        @pl.when(group > 0)
        def _(n=n, tiles=tiles):
            base[n, :tile], base[n, tile:] = tiles


def gram(table, mine, other):
    tokens, depth = mine.shape
    n = table.shape[1]
    tile = depth // (NY * NZ * 2)
    half = NZ // 2
    cols = [
        pl.BlockSpec((tokens, tile), lambda s, tab, i=i: (0, tab[0, NZ * s + i])) for i in range(NZ)
    ]
    rows = pl.BlockSpec((tokens, 4 * tile), lambda s, tab: (0, tab[3, 0]))
    fixed = pl.BlockSpec((half, 2 * tile, tile), lambda s, tab: (0, 0, 0))
    moving = pl.BlockSpec((NZ, 2 * tile, tile), lambda s, tab: (jnp.maximum(s - 1, 0), 0, 0))
    shape = lambda n, kind: jax.ShapeDtypeStruct((n, 2 * tile, tile), kind)
    return pl.pallas_call(
        gram_body,
        grid_spec=pltpu.PrefetchScalarGridSpec(
            num_scalar_prefetch=1,
            grid=(n // NZ,),
            in_specs=cols + cols + [rows, rows],
            out_specs=[fixed, fixed, moving],
            scratch_shapes=[pltpu.VMEM((4, tile, 2 * tokens), bf16)],
        ),
        out_shape=[shape(half, bf16), shape(half, bf16), shape(n - NZ, f32)],
        cost_estimate=pl.CostEstimate(
            flops=8 * tokens * 2 * tile * tile * n,
            bytes_accessed=8 * n * tokens * tile * 2,
            transcendentals=0,
        ),
        name="gram",
    )(table, *[mine] * NZ, *[other] * NZ, mine, other)


def project_body(slots, piece, fresh, table, *refs):
    out = refs[-1]
    ma, mb = refs[:slots], refs[slots : 2 * slots]
    left, right = [], []
    for w in refs[2 * slots : -1 if fresh else -2]:
        if w.shape[2] == piece:
            side = left if len(left) == len(right) else right
            side += [w[i] for i in range(w.shape[0])]
        else:
            left += [w[i, :, :piece] for i in range(w.shape[0])]
            right += [w[i, :, piece:] for i in range(w.shape[0])]
    spans = [slice(0, piece), slice(piece, 2 * piece), slice(2 * piece, 2 * piece + HEAD)]
    for core, tokens in ((0, ma), (1, mb)):
        sums = [0.0 if fresh else refs[-2][core, :, span] for span in spans]
        for x, w0, w1 in zip(tokens, left, right):
            x = x[...]
            kt = [w0[piece:], w1[piece:]]
            kt = jnp.concatenate(kt * (HEAD // (2 * kt[0].shape[0])), axis=0)
            sums[0] += jnp.dot(x, w0[:piece], preferred_element_type=f32)
            sums[1] += jnp.dot(x, w1[:piece], preferred_element_type=f32)
            sums[2] += lax.dot_general(x, kt, (((1,), (1,)), ((), ())), preferred_element_type=f32)
        for span, value in zip(spans, sums):
            out[core, :, span] = value


def project(piece, table, mine, other, weights, sofar=None):
    tokens = mine.shape[0]
    slots = table.shape[0]
    at = [pl.BlockSpec((tokens, piece), lambda s, tab, n=n: (0, tab[n])) for n in range(slots)]
    full = lambda shape: pl.BlockSpec(shape, lambda s, tab: (0, 0, 0))
    whole = (2, tokens, 2 * piece + HEAD)
    fresh = sofar is None
    return pl.pallas_call(
        functools.partial(project_body, slots, piece, fresh),
        grid_spec=pltpu.PrefetchScalarGridSpec(
            num_scalar_prefetch=1,
            grid=(1,),
            in_specs=at + at + [full(w.shape) for w in weights] + ([] if fresh else [full(whole)]),
            out_specs=full(whole),
        ),
        out_shape=jax.ShapeDtypeStruct(whole, f32),
        cost_estimate=pl.CostEstimate(
            flops=8 * tokens * piece * piece * slots,
            bytes_accessed=slots * 8 * tokens * piece + 8 * tokens * piece,
            transcendentals=0,
        ),
        name="project",
    )(table, *[mine] * slots, *[other] * slots, *weights, *([] if fresh else [sofar]))


def rope_body(at, a, b, cosine, sine, queries, keys):
    even = lax.broadcasted_iota(jnp.int32, cosine.shape, 1) % 2 == 0
    width, part = queries.shape[1], keys.shape[0]
    for start in range(0, width + HEAD, HEAD):
        x = a[0, :, start : start + HEAD] + b[:, start : start + HEAD]
        swapped = jnp.where(even, pltpu.roll(x, HEAD - 1, 1), pltpu.roll(x, 1, 1))
        x = x * cosine[...] + swapped * sine[...]
        if start < width:
            queries[:, start : start + HEAD] = x.astype(bf16)
        else:
            x = x.T
            chosen = x[:part]
            for n in range(1, HEAD // part):
                chosen = jnp.where(at[0] == n, x[n * part : (n + 1) * part], chosen)
            keys[...] = chosen.astype(bf16)


def rope(at, part, a, b, cosine, sine):
    tokens, width = b.shape
    full = lambda shape: pl.BlockSpec(shape, lambda i: (0,) * len(shape))
    shapes = [(tokens, width - HEAD), (part, tokens)]
    return pl.pallas_call(
        rope_body,
        grid=(1,),
        in_specs=[pl.BlockSpec(memory_space=pltpu.SMEM), full((1, tokens, width))]
        + [full(x.shape) for x in (b, cosine, sine)],
        out_specs=[full(shape) for shape in shapes],
        out_shape=[jax.ShapeDtypeStruct(shape, bf16) for shape in shapes],
        compiler_params=pltpu.CompilerParams(vmem_limit_bytes=12 * 2**20),
        name="rope",
    )(at, a, b, cosine, sine)


def assemble_body(scale, slots, own, r0, r1, extra, out):
    tile = out.shape[1]

    def put(n, value):
        out[pl.ds(pl.multiple_of(slots[n] * tile, tile), tile), :] = value * scale

    put(0, r1[...].astype(f32).T)
    put(1, extra[...])
    put(2, r0[...].astype(f32).T)
    put(3, own[:tile])
    put(4, own[tile:])


def assemble(scale, slots, own, r0, r1, extra):
    tile = own.shape[1]
    return pl.pallas_call(
        functools.partial(assemble_body, scale),
        in_specs=[pl.BlockSpec(memory_space=pltpu.SMEM)] + [pl.BlockSpec(memory_space=pltpu.VMEM)] * 4,
        out_shape=jax.ShapeDtypeStruct((4 * tile, tile), f32),
        compiler_params=pltpu.CompilerParams(vmem_limit_bytes=12 * 2**20),
        name="assemble",
    )(slots, own, r0, r1, extra)


def row_pair(t, c):
    u, m = t // 4, t % 4
    p = (t + (c > u)) % 2
    return jnp.where(c == u, m, p), jnp.where(c == u, (m + 1) % 4, p + 2)


def partner_moves(q):
    moves = []
    for t in range(NY * NZ * 2):
        for c in range(NC):
            u, m = t // 4, t % 4
            if c == u:
                r = (m + 1) % 4 if q == 0 else m
            else:
                r = (t + (c > u)) % 2 + 2 * ((q + m // 2) % 2)
            moves.append((t * NC + c, (4 * c + r) * NC + u))
    return moves


def shards(hidden, norm_gain, token_ids, owner, query_store, key_store):
    y, z, k = lax.axis_index("y"), lax.axis_index("zl"), lax.axis_index("k")
    column = lax.axis_index("x") * 2 + lax.axis_index("zh")
    root = owner[0]
    root_z, root_y, root_k = root // 8, (root // 2) % 4, root % 2

    tokens, depth = hidden.shape
    half = depth // 2
    piece = half // (NY * NZ)
    qwidth, kwidth = query_store.shape[2], key_store.shape[2]
    h = NZ // 2
    here = root_k == k

    q = query_store[0]
    kt = key_store[0].T

    def chip(rel):
        return (y + rel) % NY

    def block(core, rel):
        return pack(core * NY + chip(rel), q, kt)

    step_y = (y - root_y) % NY
    away, k1 = together((block(1 - k, 2), k))
    there, home = send(away, "k", 1), block(k1, 2)
    far0, far1, k2, here = together(
        (jnp.where(here, home[0], there[0]), jnp.where(here, home[1], there[1]), k, here)
    )
    a = send(far0, "y", 1)
    b = send(far1, "y", -1)
    others = [block(1 - k2, rel) for rel in (1, 3)]
    others, later_hidden, k3 = together((others, hidden, k2))
    others = [send(x, "k", 1) for x in others]
    theirs = send(later_hidden, "k", 1)
    others.append(send(block(1 - k3, 0), "k", 1))
    up, down, own = (
        jnp.where(here, block(k3, rel), x) for rel, x in zip((1, 3, 0), others)
    )
    up = jnp.where(step_y == 1, a[None], up)
    down = jnp.where(step_y == 3, b[None], down)
    up, down, gain, ours = together((up, down, norm_gain, hidden))
    c = send(up, "y", 1)
    d = send(down, "y", -1)

    mine = normalize(ours, gain)
    other = normalize(theirs, gain)

    zs = (z + jnp.arange(NZ)) % NZ
    t = (zs[None] * (2 * NY) + chip(jnp.array([2, 1, 3, 0])[:, None]) * 2 + k).reshape(-1)
    r0, r1 = row_pair(t, column)
    table = jnp.stack([t, r0, r1, jnp.full_like(t, column)]).astype(jnp.int32)
    p_low, p_high, base = gram(table, mine, other)

    tile = depth // (NY * NZ * 2)
    both = [lax.dynamic_slice_in_dim(x, (4 * column + k) * tile, 3 * tile, 1) for x in (mine, other)]
    extra = sum(across(x[:, :tile], x[:, 2 * tile :]) for x in both)

    def butterfly(extra, axis, bit):
        return extra + swap(extra.astype(bf16), axis, bit).astype(f32)

    extra = butterfly(extra, "zl", 1)
    p_low, p_high, base, extra, own, step_y = together((p_low, p_high, base, extra, own, step_y))
    low = lax.broadcasted_iota(jnp.int32, (2, 1, 1), 0) == 0
    from_c = (step_y == 1) | ((step_y == 2) & low)
    quarter = jnp.where(step_y == 0, own, jnp.where(from_c, c, d))
    side = quarter[:, h * piece :].reshape(2, 2, kwidth // 2, 2, piece)
    side = side.transpose(0, 3, 2, 1, 4).reshape(NZ, kwidth // 2, 2 * piece)
    quarter = quarter[:, : h * piece].reshape(NZ, piece, qwidth)
    quarter = jnp.concatenate([quarter, side], axis=1)
    p_low, p_high, quarter = together((p_low, p_high, quarter))

    ga = send(p_low, "y", 1)
    gb = send(p_high, "y", -1)
    quarter = quarter.reshape(2, h, *quarter.shape[1:])
    kept = swap(pick(quarter, 1 - z % 2), "zl", 1)
    first = lax.broadcasted_iota(jnp.int32, (2, 1, 1, 1), 0) == 0
    shape = (2, h, 2 * tile, tile)
    up = base[:NZ].reshape(shape) + jnp.where(first, ga.astype(f32)[None], 0.0)
    down = base[NZ : 2 * NZ].reshape(shape) + jnp.where(first, 0.0, gb.astype(f32)[None])
    kept = jnp.where(z == root_z, pick(quarter, z % 2), kept)
    extra = butterfly(extra, "zl", 2)
    up, down, kept, extra = together((up.astype(bf16), down.astype(bf16), kept, extra))
    gc = send(up, "y", 1).reshape(NZ, 2 * tile, tile)
    gd = send(down, "y", -1).reshape(NZ, 2 * tile, tile)
    kept = jnp.where(z // 2 == root_z // 2, kept, swap(kept, "zl", 2))
    extra = butterfly(extra, "y", 1)
    total = [base[2 * NZ + s] + gc[s].astype(f32) + gd[s].astype(f32) for s in range(NZ)]
    hess, rest = total[0], [x.astype(bf16) for x in total[1:]]
    kept, hess, rest, extra = together((kept, hess, rest, extra))

    pairs = jnp.concatenate([2 * (z % 2) + jnp.arange(2), 2 * (1 - z % 2) + jnp.arange(2)])

    def depth_tiles(rel):
        return (k * NY * NZ + chip(rel) * NZ + pairs).astype(jnp.int32)

    product = functools.partial(project, piece)
    crossed = swap(kept, "zl", 1)
    left0, right0 = send(kept, "y", 1), send(kept, "y", -1)
    cosine, sine = turns(positions(token_ids))
    extra = butterfly(extra, "y", 2)
    crossed, left0, right0, rest, extra, cosine, sine = together(
        (crossed, left0, right0, rest, extra, cosine, sine)
    )
    left1, right1 = send(crossed, "y", 1), send(crossed, "y", -1)
    parts = [send(rest[1], "zl", 2)]
    raw = product(depth_tiles(0), mine, other, [kept, crossed])
    left0, left1, right1, parts, raw, rest = together((left0, left1, right1, parts, raw, rest))
    fl, fr = send(left0, "y", 1), send(right1, "y", -1)
    parts += [send(rest[0], "zl", 1), send(rest[2], "zl", 3)]
    sides = jnp.concatenate([depth_tiles(3), depth_tiles(1)])
    raw = product(sides, mine, other, [left0, left1, right0, right1], raw)
    fl, fr, parts, raw = together((fl, fr, parts, raw))

    for x in parts:
        hess = hess + x.astype(f32)
    t = z * (2 * NY) + y * 2 + k
    u, m = t // 4, t % 4
    diagonal = column == u
    r0, r1 = row_pair(t, column)
    tiles, raw = together((hess.astype(bf16), raw))
    tiles = [tiles[:tile], tiles[tile:]]
    mirrored = []
    for n in (0, 1):
        second = jnp.where(diagonal, 1, (n + m // 2) % 2) == 1
        mirrored.append(lax.ppermute(jnp.where(second, tiles[1], tiles[0]), ALL, partner_moves(n)))
    missing = 1 - r0 % 2
    slot0 = jnp.where(diagonal, (m + 3) % 4, missing + 2 * ((m // 2) % 2))
    slot1 = jnp.where(diagonal, (m + 2) % 4, missing + 2 * ((m // 2 + 1) % 2))
    slots = jnp.stack([slot1, jnp.where(diagonal, slot1, r0), slot0, r0, r1]).astype(jnp.int32)
    extra = jnp.where(m < 2, extra.T, extra)

    raw = product(depth_tiles(2), mine, other, [fl, fr], raw)
    all_tokens = tokens * NY * NZ * 2
    hessian = assemble(2.0 / all_tokens, slots, hess, mirrored[0], mirrored[1], extra)
    at = ((column * kwidth) % HEAD) // kwidth
    queries, keys = rope(at.reshape(1), kwidth, raw, send(raw[1], "k", 1), cosine, sine)
    return (queries, keys.T, hessian)


def solution(mesh):
    fine = Mesh(mesh.devices.reshape(NZ, NY, 2, 4, 2), ALL)
    placed = (P(TOK, None), P(), P(TOK), P(), P(TOK, None, COL), P(TOK, None, COL))
    return jax.shard_map(
        shards,
        mesh=fine,
        in_specs=placed,
        out_specs=(P(TOK, COL), P(TOK, COL), P(COL, TOK)),
        check_vma=False,
    )
```

```python
import functools

import jax
import jax.numpy as jnp
from jax import lax
from jax.experimental import pallas as pl
from jax.experimental.pallas import tpu as pltpu
from jax.sharding import Mesh, PartitionSpec as P

HEAD = 128
SEQ = 128


begin_token = 128000
rope_base = 500000.0

NY, NZ, NC = 4, 4, 8
TOK = ("zl", "y", "k")
COL = ("x", "zh")
ALL = TOK + COL
SIZES = {"y": NY, "zl": NZ, "k": 2}
f32, bf16 = jnp.float32, jnp.bfloat16


def send(array, axis, shift):
    n = SIZES[axis]
    return lax.ppermute(array, axis, [(i, (i + shift) % n) for i in range(n)])


def swap(array, axis, bit):
    return lax.ppermute(array, axis, [(i, i ^ bit) for i in range(SIZES[axis])])


together = lax.optimization_barrier


def pick(array, index):
    return lax.dynamic_index_in_dim(array, index, 0, keepdims=False)


def positions(token_ids):
    samples = token_ids.reshape(-1, SEQ)
    index = jnp.arange(SEQ, dtype=jnp.int32)
    starts = jnp.where(samples == begin_token, index[None, :], 0)
    seen = index[None, :] <= index[:, None]
    latest = jnp.max(jnp.where(seen[None], starts[:, None, :], 0), axis=2)
    return (index[None, :] - latest).reshape(-1)


def turns(place):
    dims = jnp.arange(HEAD, dtype=jnp.int32)
    pair = (dims // 2).astype(f32)
    freq = jnp.power(f32(rope_base), -2.0 * pair / HEAD)
    angle = place.astype(f32)[:, None] * freq[None, :]
    sign = jnp.where(dims % 2 == 0, -1.0, 1.0).astype(f32)
    return jnp.cos(angle), jnp.sin(angle) * sign[None, :]


def normalize(hidden, norm_gain):
    wide = hidden.astype(f32)
    meansq = jnp.mean(wide * wide, axis=-1, keepdims=True)
    return (wide * lax.rsqrt(meansq + 1e-05) * norm_gain[None, :]).astype(bf16)


def pack_body(table, q, kt, out):
    n = q.shape[0]
    out[0, :n] = q[...]
    out[0, n:] = kt[...]


def pack(at, q, kt):
    width, side = q.shape[1], kt.shape[0]
    n = q.shape[0] // (4 * NY)
    return pl.pallas_call(
        pack_body,
        grid_spec=pltpu.PrefetchScalarGridSpec(
            num_scalar_prefetch=1,
            grid=(2,),
            in_specs=[
                pl.BlockSpec((n, width), lambda p, tab: (2 * tab[0] + p, 0)),
                pl.BlockSpec((side, width), lambda p, tab: (0, 2 * tab[0] + p)),
            ],
            out_specs=pl.BlockSpec((1, n + side, width), lambda p, tab: (p, 0, 0)),
        ),
        out_shape=jax.ShapeDtypeStruct((2, n + side, width), bf16),
        cost_estimate=pl.CostEstimate(
            flops=0, bytes_accessed=8 * (n + side) * width, transcendentals=0
        ),
        name="pack",
    )(at.reshape(1).astype(jnp.int32), q, kt)


def across(left, right):
    return lax.dot_general(left, right, (((0,), (0,)), ((), ())), preferred_element_type=f32)


def gram_body(table, *refs):
    cas, cbs = refs[:NZ], refs[NZ : 2 * NZ]
    ra, rb, low, high, base, turned = refs[2 * NZ :]
    group = pl.program_id(0)
    half = NZ // 2
    tokens, tile = cas[0].shape

    @pl.when(group == 0)
    def _():
        for n in range(4):
            span = slice(n * tile, (n + 1) * tile)
            turned[n, :, :tokens] = ra[:, span].T
            turned[n, :, tokens:] = rb[:, span].T

    for n in range(NZ):
        columns = jnp.concatenate([cas[n][...], cbs[n][...]], axis=0)
        rows = [turned[table[i, NZ * group + n]] for i in (1, 2)]
        tiles = [jnp.dot(x, columns, preferred_element_type=f32) for x in rows]
        far, at = (low, n) if n < half else (high, n - half)

        @pl.when(group == 0)
        def _(far=far, at=at, tiles=tiles):
            far[at, :tile], far[at, tile:] = (x.astype(bf16) for x in tiles)

        @pl.when(group > 0)
        def _(n=n, tiles=tiles):
            base[n, :tile], base[n, tile:] = tiles


def gram(table, mine, other):
    tokens, depth = mine.shape
    n = table.shape[1]
    tile = depth // (NY * NZ * 2)
    half = NZ // 2
    cols = [
        pl.BlockSpec((tokens, tile), lambda s, tab, i=i: (0, tab[0, NZ * s + i])) for i in range(NZ)
    ]
    rows = pl.BlockSpec((tokens, 4 * tile), lambda s, tab: (0, tab[3, 0]))
    fixed = pl.BlockSpec((half, 2 * tile, tile), lambda s, tab: (0, 0, 0))
    moving = pl.BlockSpec((NZ, 2 * tile, tile), lambda s, tab: (jnp.maximum(s - 1, 0), 0, 0))
    shape = lambda n, kind: jax.ShapeDtypeStruct((n, 2 * tile, tile), kind)
    return pl.pallas_call(
        gram_body,
        grid_spec=pltpu.PrefetchScalarGridSpec(
            num_scalar_prefetch=1,
            grid=(n // NZ,),
            in_specs=cols + cols + [rows, rows],
            out_specs=[fixed, fixed, moving],
            scratch_shapes=[pltpu.VMEM((4, tile, 2 * tokens), bf16)],
        ),
        out_shape=[shape(half, bf16), shape(half, bf16), shape(n - NZ, f32)],
        cost_estimate=pl.CostEstimate(
            flops=8 * tokens * 2 * tile * tile * n,
            bytes_accessed=8 * n * tokens * tile * 2,
            transcendentals=0,
        ),
        name="gram",
    )(table, *[mine] * NZ, *[other] * NZ, mine, other)


def project_body(slots, piece, fresh, table, *refs):
    outs = refs[-2:]
    ma, mb = refs[:slots], refs[slots : 2 * slots]
    left, right = [], []
    for w in refs[2 * slots : -2 if fresh else -4]:
        if w.shape[2] == piece:
            side = left if len(left) == len(right) else right
            side += [w[i] for i in range(w.shape[0])]
        else:
            left += [w[i, :, :piece] for i in range(w.shape[0])]
            right += [w[i, :, piece:] for i in range(w.shape[0])]
    spans = [slice(0, piece), slice(piece, 2 * piece), slice(2 * piece, 2 * piece + HEAD)]
    for core, tokens in ((0, ma), (1, mb)):
        sums = [0.0 if fresh else refs[-4 + core][:, span] for span in spans]
        for x, w0, w1 in zip(tokens, left, right):
            x = x[...]
            kt = [w0[piece:], w1[piece:]]
            kt = jnp.concatenate(kt * (HEAD // (2 * kt[0].shape[0])), axis=0)
            sums[0] += jnp.dot(x, w0[:piece], preferred_element_type=f32)
            sums[1] += jnp.dot(x, w1[:piece], preferred_element_type=f32)
            sums[2] += lax.dot_general(x, kt, (((1,), (1,)), ((), ())), preferred_element_type=f32)
        for span, value in zip(spans, sums):
            outs[core][:, span] = value


def project(piece, table, mine, other, weights, sofar=None):
    tokens = mine.shape[0]
    slots = table.shape[0]
    at = [pl.BlockSpec((tokens, piece), lambda s, tab, n=n: (0, tab[n])) for n in range(slots)]
    full = lambda shape: pl.BlockSpec(shape, lambda s, tab: (0, 0, 0))
    whole = (tokens, 2 * piece + HEAD)
    both = pl.BlockSpec(whole, lambda s, tab: (0, 0))
    fresh = sofar is None
    return pl.pallas_call(
        functools.partial(project_body, slots, piece, fresh),
        grid_spec=pltpu.PrefetchScalarGridSpec(
            num_scalar_prefetch=1,
            grid=(1,),
            in_specs=at + at + [full(w.shape) for w in weights] + ([] if fresh else [both] * 2),
            out_specs=[both] * 2,
        ),
        out_shape=[jax.ShapeDtypeStruct(whole, f32)] * 2,
        cost_estimate=pl.CostEstimate(
            flops=8 * tokens * piece * piece * slots,
            bytes_accessed=slots * 8 * tokens * piece + 8 * tokens * piece,
            transcendentals=0,
        ),
        name="project",
    )(table, *[mine] * slots, *[other] * slots, *weights, *([] if fresh else sofar))


def rope_body(at, a, b, cosine, sine, queries, keys):
    even = lax.broadcasted_iota(jnp.int32, cosine.shape, 1) % 2 == 0
    width, part = queries.shape[1], keys.shape[0]
    for start in range(0, width + HEAD, HEAD):
        x = a[:, start : start + HEAD] + b[:, start : start + HEAD]
        swapped = jnp.where(even, pltpu.roll(x, HEAD - 1, 1), pltpu.roll(x, 1, 1))
        x = x * cosine[...] + swapped * sine[...]
        if start < width:
            queries[:, start : start + HEAD] = x.astype(bf16)
        else:
            x = x.T
            chosen = x[:part]
            for n in range(1, HEAD // part):
                chosen = jnp.where(at[0] == n, x[n * part : (n + 1) * part], chosen)
            keys[...] = chosen.astype(bf16)


def rope(at, part, a, b, cosine, sine):
    tokens, width = b.shape
    full = lambda shape: pl.BlockSpec(shape, lambda i: (0,) * len(shape))
    shapes = [(tokens, width - HEAD), (part, tokens)]
    return pl.pallas_call(
        rope_body,
        grid=(1,),
        in_specs=[pl.BlockSpec(memory_space=pltpu.SMEM), full((tokens, width))]
        + [full(x.shape) for x in (b, cosine, sine)],
        out_specs=[full(shape) for shape in shapes],
        out_shape=[jax.ShapeDtypeStruct(shape, bf16) for shape in shapes],
        compiler_params=pltpu.CompilerParams(vmem_limit_bytes=12 * 2**20),
        name="rope",
    )(at, a, b, cosine, sine)


def assemble_body(scale, slots, own, r0, r1, extra, out):
    tile = out.shape[1]

    def put(n, value):
        out[pl.ds(pl.multiple_of(slots[n] * tile, tile), tile), :] = value * scale

    put(0, r1[...].astype(f32).T)
    put(1, extra[...])
    put(2, r0[...].astype(f32).T)
    put(3, own[:tile])
    put(4, own[tile:])


def assemble(scale, slots, own, r0, r1, extra):
    tile = own.shape[1]
    return pl.pallas_call(
        functools.partial(assemble_body, scale),
        in_specs=[pl.BlockSpec(memory_space=pltpu.SMEM)] + [pl.BlockSpec(memory_space=pltpu.VMEM)] * 4,
        out_shape=jax.ShapeDtypeStruct((4 * tile, tile), f32),
        compiler_params=pltpu.CompilerParams(vmem_limit_bytes=12 * 2**20),
        name="assemble",
    )(slots, own, r0, r1, extra)


def row_pair(t, c):
    u, m = t // 4, t % 4
    p = (t + (c > u)) % 2
    return jnp.where(c == u, m, p), jnp.where(c == u, (m + 1) % 4, p + 2)


def partner_moves(q):
    moves = []
    for t in range(NY * NZ * 2):
        for c in range(NC):
            u, m = t // 4, t % 4
            if c == u:
                r = (m + 1) % 4 if q == 0 else m
            else:
                r = (t + (c > u)) % 2 + 2 * ((q + m // 2) % 2)
            moves.append((t * NC + c, (4 * c + r) * NC + u))
    return moves


def shards(hidden, norm_gain, token_ids, owner, query_store, key_store):
    y, z, k = lax.axis_index("y"), lax.axis_index("zl"), lax.axis_index("k")
    column = lax.axis_index("x") * 2 + lax.axis_index("zh")
    root = owner[0]
    root_z, root_y, root_k = root // 8, (root // 2) % 4, root % 2

    tokens, depth = hidden.shape
    half = depth // 2
    piece = half // (NY * NZ)
    qwidth, kwidth = query_store.shape[2], key_store.shape[2]
    h = NZ // 2
    here = root_k == k

    q = query_store[0]
    kt = key_store[0].T

    def chip(rel):
        return (y + rel) % NY

    def block(core, rel):
        return pack(core * NY + chip(rel), q, kt)

    step_y = (y - root_y) % NY
    away, k1 = together((block(1 - k, 2), k))
    there, home = send(away, "k", 1), block(k1, 2)
    far0, far1, k2, here = together(
        (jnp.where(here, home[0], there[0]), jnp.where(here, home[1], there[1]), k, here)
    )
    a = send(far0, "y", 1)
    b = send(far1, "y", -1)
    others = [block(1 - k2, rel) for rel in (1, 3)]
    others, later_hidden, k3 = together((others, hidden, k2))
    others = [send(x, "k", 1) for x in others]
    theirs = send(later_hidden, "k", 1)
    others.append(send(block(1 - k3, 0), "k", 1))
    up, down, own = (
        jnp.where(here, block(k3, rel), x) for rel, x in zip((1, 3, 0), others)
    )
    up = jnp.where(step_y == 1, a[None], up)
    down = jnp.where(step_y == 3, b[None], down)
    up, down, gain, ours = together((up, down, norm_gain, hidden))
    c = send(up, "y", 1)
    d = send(down, "y", -1)

    mine = normalize(ours, gain)
    other = normalize(theirs, gain)

    zs = (z + jnp.arange(NZ)) % NZ
    t = (zs[None] * (2 * NY) + chip(jnp.array([2, 1, 3, 0])[:, None]) * 2 + k).reshape(-1)
    r0, r1 = row_pair(t, column)
    table = jnp.stack([t, r0, r1, jnp.full_like(t, column)]).astype(jnp.int32)
    p_low, p_high, base = gram(table, mine, other)

    tile = depth // (NY * NZ * 2)
    both = [lax.dynamic_slice_in_dim(x, (4 * column + k) * tile, 3 * tile, 1) for x in (mine, other)]
    extra = sum(across(x[:, :tile], x[:, 2 * tile :]) for x in both)

    def butterfly(extra, axis, bit):
        return extra + swap(extra.astype(bf16), axis, bit).astype(f32)

    extra = butterfly(extra, "zl", 1)
    p_low, p_high, base, extra, own, step_y = together((p_low, p_high, base, extra, own, step_y))
    low = lax.broadcasted_iota(jnp.int32, (2, 1, 1), 0) == 0
    from_c = (step_y == 1) | ((step_y == 2) & low)
    quarter = jnp.where(step_y == 0, own, jnp.where(from_c, c, d))
    side = quarter[:, h * piece :].reshape(2, 2, kwidth // 2, 2, piece)
    side = side.transpose(0, 3, 2, 1, 4).reshape(NZ, kwidth // 2, 2 * piece)
    quarter = quarter[:, : h * piece].reshape(NZ, piece, qwidth)
    quarter = jnp.concatenate([quarter, side], axis=1)
    p_low, p_high, quarter = together((p_low, p_high, quarter))

    ga = send(p_low, "y", 1)
    gb = send(p_high, "y", -1)
    quarter = quarter.reshape(2, h, *quarter.shape[1:])
    kept = swap(pick(quarter, 1 - z % 2), "zl", 1)
    first = lax.broadcasted_iota(jnp.int32, (2, 1, 1, 1), 0) == 0
    shape = (2, h, 2 * tile, tile)
    up = base[:NZ].reshape(shape) + jnp.where(first, ga.astype(f32)[None], 0.0)
    down = base[NZ : 2 * NZ].reshape(shape) + jnp.where(first, 0.0, gb.astype(f32)[None])
    kept = jnp.where(z == root_z, pick(quarter, z % 2), kept)
    extra = butterfly(extra, "zl", 2)
    up, down, kept, extra = together((up.astype(bf16), down.astype(bf16), kept, extra))
    gc = send(up, "y", 1).reshape(NZ, 2 * tile, tile)
    gd = send(down, "y", -1).reshape(NZ, 2 * tile, tile)
    kept = jnp.where(z // 2 == root_z // 2, kept, swap(kept, "zl", 2))
    extra = butterfly(extra, "y", 1)
    total = [base[2 * NZ + s] + gc[s].astype(f32) + gd[s].astype(f32) for s in range(NZ)]
    hess, rest = total[0], [x.astype(bf16) for x in total[1:]]
    kept, hess, rest, extra = together((kept, hess, rest, extra))

    pairs = jnp.concatenate([2 * (z % 2) + jnp.arange(2), 2 * (1 - z % 2) + jnp.arange(2)])

    def depth_tiles(rel):
        return (k * NY * NZ + chip(rel) * NZ + pairs).astype(jnp.int32)

    product = functools.partial(project, piece)
    crossed = swap(kept, "zl", 1)
    left0, right0 = send(kept, "y", 1), send(kept, "y", -1)
    cosine, sine = turns(positions(token_ids))
    extra = butterfly(extra, "y", 2)
    crossed, left0, right0, rest, extra, cosine, sine = together(
        (crossed, left0, right0, rest, extra, cosine, sine)
    )
    left1, right1 = send(crossed, "y", 1), send(crossed, "y", -1)
    parts = [send(rest[1], "zl", 2)]
    raw = product(depth_tiles(0), mine, other, [kept, crossed])
    left0, left1, right1, parts, raw, rest = together((left0, left1, right1, parts, raw, rest))
    fl, fr = send(left0, "y", 1), send(right1, "y", -1)
    parts += [send(rest[0], "zl", 1), send(rest[2], "zl", 3)]
    sides = jnp.concatenate([depth_tiles(3), depth_tiles(1)])
    raw = product(sides, mine, other, [left0, left1, right0, right1], raw)
    fl, fr, parts, raw = together((fl, fr, parts, raw))

    for x in parts:
        hess = hess + x.astype(f32)
    t = z * (2 * NY) + y * 2 + k
    u, m = t // 4, t % 4
    diagonal = column == u
    r0, r1 = row_pair(t, column)
    tiles, raw = together((hess.astype(bf16), raw))
    tiles = [tiles[:tile], tiles[tile:]]
    mirrored = []
    for n in (0, 1):
        second = jnp.where(diagonal, 1, (n + m // 2) % 2) == 1
        mirrored.append(lax.ppermute(jnp.where(second, tiles[1], tiles[0]), ALL, partner_moves(n)))
    missing = 1 - r0 % 2
    slot0 = jnp.where(diagonal, (m + 3) % 4, missing + 2 * ((m // 2) % 2))
    slot1 = jnp.where(diagonal, (m + 2) % 4, missing + 2 * ((m // 2 + 1) % 2))
    slots = jnp.stack([slot1, jnp.where(diagonal, slot1, r0), slot0, r0, r1]).astype(jnp.int32)
    extra = jnp.where(m < 2, extra.T, extra)

    raw = product(depth_tiles(2), mine, other, [fl, fr], raw)
    all_tokens = tokens * NY * NZ * 2
    hessian = assemble(2.0 / all_tokens, slots, hess, mirrored[0], mirrored[1], extra)
    at = ((column * kwidth) % HEAD) // kwidth
    queries, keys = rope(at.reshape(1), kwidth, raw[0], send(raw[1], "k", 1), cosine, sine)
    return (queries, keys.T, hessian)


def solution(mesh):
    fine = Mesh(mesh.devices.reshape(NZ, NY, 2, 4, 2), ALL)
    placed = (P(TOK, None), P(), P(TOK), P(), P(TOK, None, COL), P(TOK, None, COL))
    return jax.shard_map(
        shards,
        mesh=fine,
        in_specs=placed,
        out_specs=(P(TOK, COL), P(TOK, COL), P(COL, TOK)),
        check_vma=False,
    )
```
